32 devices in a mesh: groups: 2 (over x), row: 8 (over z, y), col: 2 (over core).
Axes of the slice: x: 2, y: 2, z: 4, core: 2. Of those that a mesh axis runs over, the one named last changes fastest.
Arguments:
- queries: bfloat16 [4096, 2560], P(('groups', 'row', 'col')), parts along dimension 0, may hold values from -32 to 32
- keys: bfloat16 [4096, 2560], P(('groups', 'row', 'col')), parts along dimension 0, may hold values from -6 to 6
- values: bfloat16 [4096, 2560], P(('groups', 'row', 'col')), parts along dimension 0, may hold values from -6 to 6
- pattern: int32 [16, 5], P('groups'), parts along dimension 0, may hold values from 0 to 1, as said below
Outputs:
- attended: bfloat16 [4096, 2560], P(('groups', 'row', 'col')), parts along dimension 0
The draws below stay inside these ranges and needn't reach their ends.
There are 2 independent parts, one for each index of `groups`. The reference program is written for one: setup_inputs(seed, part) draws one part's arguments, and reference() takes and returns one part's arrays. A program takes and returns all parts, laid end to end along the dimension named above; each array names one. Nothing has to cross between parts.
Inputs may be any that keep to these rules, and one draw needn't show every extreme that they name: pattern[r, 0] is 1; pattern[r, j] is 0 where r + off_j lies outside 0 .. 7, or where off_j is -1 or +1 and r + off_j lies in another band of 4 tile rows.
All inputs are finite; a program needn't handle non-finite values.
Results may differ from the reference program's by a relative error of at most 0.0045.
Values may be sent and summed in bfloat16 or wider, within the bound.
No kernel may reach another device: no remote copies, remote signals or barrier semaphores. Data moves between devices by JAX's collectives and lax.ppermute only.
A program may use at most 64 MiB of HBM per device.

```python
import math
import jax
import jax.numpy as jnp
from jax import lax

HEADS = 20
HD = 128
TILE_H = 4
WIDTH = 2560
TILE_ROWS = 8
TOKENS = 2048


def shared_draw(key):
    base = jax.random.fold_in(key, 17)
    first = jax.random.fold_in(base, 0)
    third = jax.random.fold_in(base, 2)
    width = HEADS * HD
    shape = (TOKENS, width)
    keys_all = jnp.clip(jax.random.normal(first, shape, jnp.float32), -6.0, 6.0)
    queries_all = jnp.clip(jax.random.normal(third, shape, jnp.float32), -6.0, 6.0)
    return (queries_all, keys_all)


def draw_queries(key, part):
    return shared_draw(key)[0].astype(jnp.bfloat16)


def draw_keys(key, part):
    return shared_draw(key)[1].astype(jnp.bfloat16)


def draw_pattern(key, part):
    first, second = jax.random.split(jax.random.fold_in(key, 29))
    row_numbers = jnp.arange(TILE_ROWS, dtype=jnp.int32)[:, None]
    offsets = jnp.array([0, -1, 1, -TILE_H, TILE_H], jnp.int32)[None, :]
    target = row_numbers + offsets
    inside = (target >= 0) & (target < TILE_ROWS)
    same_band = (jnp.abs(offsets) != 1) | (target // TILE_H == row_numbers // TILE_H)
    appetite = jax.random.randint(first, (TILE_ROWS, 1), 0, 5)
    rolls = jax.random.randint(second, (TILE_ROWS, 5), 0, 4)
    chosen = (rolls < appetite) & inside & same_band | (offsets == 0)
    return chosen.astype(jnp.int32)


def steps_of(own_key, dims, shards, smallest, high):
    def one(dim, parts):
        draws = jax.random.uniform(jax.random.fold_in(jax.random.fold_in(own_key, 6), dim), (parts,), jnp.float32, smallest / len(shards), high / len(shards))
        return jnp.repeat(jnp.exp(draws), dims[dim] // parts).reshape((-1,) + (1,) * (len(dims) - dim - 1))

    factor_of = one(*shards[0])
    for cut in shards[1:]:
        factor_of = factor_of * one(*cut)
    return factor_of


def scatter_about(own_key, shape, scale, bound, cuts=(), held_as=jnp.bfloat16):
    values = scale * jax.random.normal(own_key, shape, jnp.float32)
    if cuts:
        values = values * steps_of(own_key, shape, cuts, -0.22, 0.18)
    return jnp.clip(values, -bound, bound).astype(held_as)


def setup_inputs(seed: int = 0, part: int = 0) -> dict:
    key_list = jax.random.split(jax.random.key(seed), 5)
    part_splits = jax.random.split(jax.random.fold_in(key_list[4], part), 5)
    return {
        "queries": draw_queries(jax.random.fold_in(jax.random.fold_in(key_list[4], part), 71), part),
        "keys": draw_keys(jax.random.fold_in(jax.random.fold_in(key_list[4], part), 71), part),
        "values": scatter_about(part_splits[2], (TOKENS, WIDTH), 1.0, 6.0, ((0, 16),)),
        "pattern": draw_pattern(jax.random.fold_in(jax.random.fold_in(key_list[4], part), 71), part),
    }


far_below = -1e+30

def block_terms(query_block, key_block, value_block):
    query_float = query_block.astype(jnp.float32)
    key_float = key_block.astype(jnp.float32)
    value_float = value_block.astype(jnp.float32)
    scores = jnp.einsum('qhd,khd->hqk', query_float, key_float, precision=lax.Precision.HIGHEST) * (1.0 / math.sqrt(HD))
    block_max = lax.optimization_barrier(jnp.max(scores, axis=2))
    weights = jnp.exp(scores - block_max[:, :, None])
    block_total = lax.optimization_barrier(jnp.sum(weights, axis=2))
    rounded = lax.optimization_barrier(weights.astype(jnp.bfloat16)).astype(jnp.float32)
    block_out = jnp.einsum('hqk,khd->qhd', rounded, value_float, precision=lax.Precision.HIGHEST)
    return (block_out, block_max.T, block_total.T)

def reference(queries, keys, values, pattern):
    row_tokens = TOKENS // TILE_ROWS
    query_rows = queries.reshape(TILE_ROWS, row_tokens, HEADS, HD)
    key_rows = keys.reshape(TILE_ROWS, row_tokens, HEADS, HD)
    value_rows = values.reshape(TILE_ROWS, row_tokens, HEADS, HD)
    offsets = [0, -1, 1, -TILE_H, TILE_H]

    def one_row(row_number):
        query_block = lax.dynamic_index_in_dim(query_rows, row_number, 0, keepdims=False)
        outs_list = []
        maxes_list = []
        totals_list = []
        for number in range(5):
            key_index = jnp.clip(row_number + offsets[number], 0, TILE_ROWS - 1).astype(jnp.int32)
            key_block = lax.dynamic_index_in_dim(key_rows, key_index, 0, keepdims=False)
            value_block = lax.dynamic_index_in_dim(value_rows, key_index, 0, keepdims=False)
            block_out, block_max, block_total = block_terms(query_block, key_block, value_block)
            is_live = pattern[row_number, number] == 1
            outs_list.append(jnp.where(is_live, block_out, jnp.float32(0.0)))
            maxes_list.append(jnp.where(is_live, block_max, jnp.float32(far_below)))
            totals_list.append(jnp.where(is_live, block_total, jnp.float32(0.0)))
        outs_all = jnp.stack(outs_list)
        maxes_all = jnp.stack(maxes_list)
        totals_all = jnp.stack(totals_list)
        top_max = lax.optimization_barrier(jnp.max(maxes_all, axis=0))
        factors = jnp.exp(maxes_all - top_max)
        numerator = lax.optimization_barrier(jnp.sum(factors[..., None] * outs_all, axis=0))
        denominator = lax.optimization_barrier(jnp.sum(factors * totals_all, axis=0))
        result = (numerator / denominator[..., None]).astype(jnp.bfloat16)
        return result.reshape(row_tokens, HEADS * HD)
    attended = lax.map(one_row, jnp.arange(TILE_ROWS, dtype=jnp.int32))
    return attended.reshape(TOKENS, HEADS * HD)
```

```python
import functools

import jax
import jax.numpy as jnp
from jax import lax
from jax.experimental import pallas as pl
from jax.experimental.pallas import tpu as pltpu
from jax.sharding import PartitionSpec as P

HD = 128
TILE_H = 4
OFFSETS = (0, -1, 1, -TILE_H, TILE_H)
SCALE = HD ** (-0.5) * 1.4426950408889634
FAR_BELOW = -1e30
HEADS_AT_ONCE = 4


def plan(rows):
    edges = []
    for to in range(rows):
        for number, offset in enumerate(OFFSETS):
            source = to + offset
            if offset == 0 or not 0 <= source < rows:
                continue
            if abs(offset) == 1 and source // TILE_H != to // TILE_H:
                continue
            place, up = source % TILE_H, to > source
            half = TILE_H // 2
            if abs(offset) == TILE_H:
                wanted = 0 if (place >= half) == up else 1
            elif source // 2 == to // 2:
                wanted = 2
            else:
                odd = (source // TILE_H) % 2 == 1
                wanted = 0 if up != odd else 1
            edges.append((abs(offset) != TILE_H, source, to, number, wanted))
    edges.sort()
    phases = [{}, {}, {}]
    for _, source, to, number, wanted in edges:
        order = [wanted] + list(range(3, len(phases))) + [len(phases)]
        for index in order:
            if index == len(phases):
                phases.append({})
            phase = phases[index]
            if source not in phase and all(t != to for t, _ in phase.values()):
                phase[source] = (to, number)
                break
    return phases


def scores_of(q, k_own, k_other):
    keys = jnp.concatenate([k_own, k_other], axis=0)
    return lax.dot_general(
        q, keys, (((1,), (1,)), ((), ())), preferred_element_type=jnp.float32
    ) * SCALE


def weighted(weights, v_own, v_other):
    return jnp.dot(
        weights.astype(jnp.bfloat16),
        jnp.concatenate([v_own, v_other], axis=0),
        preferred_element_type=jnp.float32,
    )


def absorb(live, head, q_ref, block, max_ref, total_ref, out_ref):
    k_own, k_other, v_own, v_other = block
    here = slice(head * HD, (head + 1) * HD)

    scores = scores_of(q_ref[:, here], k_own[:, here], k_other[:, here])
    before = max_ref[head]
    top = jnp.maximum(before, jnp.max(scores, axis=1, keepdims=True))
    weights = jnp.exp2(scores - top[:, :1])
    factor = jnp.exp2(before - top)
    max_ref[head] = top
    total_ref[head] = factor * total_ref[head] + jnp.sum(weights, axis=1, keepdims=True)
    out_ref[:, here] = factor * out_ref[:, here] + weighted(
        weights, v_own[:, here], v_other[:, here]
    )


def first_kernel(blocks, heads, live_ref, q_ref, *refs):
    kv = refs[: 4 * blocks]
    out_ref, stat_ref, max_ref, total_ref = refs[4 * blocks :]
    max_ref[...] = jnp.full_like(max_ref, FAR_BELOW)
    total_ref[...] = jnp.zeros_like(total_ref)
    out_ref[...] = jnp.zeros_like(out_ref)
    for number in range(blocks):
        block = kv[4 * number : 4 * number + 4]

        @pl.when(live_ref[number] == 1)
        def _():
            for head in range(heads):
                absorb(None, head, q_ref, block, max_ref, total_ref, out_ref)

    for head in range(heads):
        here = slice(head * HD, (head + 1) * HD)
        total = total_ref[head]
        out_ref[:, here] = out_ref[:, here] / total
        stat_ref[:, here] = max_ref[head] + jnp.log2(total)


def last_kernel(blocks, heads, live_ref, q_ref, *refs):
    kv = refs[: 4 * blocks]
    before_ref, stat_ref, out_ref, max_ref, total_ref, sum_ref = refs[4 * blocks :]
    for head in range(heads):
        here = slice(head * HD, (head + 1) * HD)
        max_ref[head] = stat_ref[:, here]
    total_ref[...] = jnp.ones_like(total_ref)
    sum_ref[...] = before_ref[...]
    for number in range(blocks):
        block = kv[4 * number : 4 * number + 4]

        @pl.when(live_ref[number] == 1)
        def _():
            for head in range(heads):
                absorb(None, head, q_ref, block, max_ref, total_ref, sum_ref)

    for head in range(heads):
        here = slice(head * HD, (head + 1) * HD)
        out_ref[:, here] = (sum_ref[:, here] / total_ref[head]).astype(out_ref.dtype)


def heads_at_once(heads):
    return max(n for n in range(1, HEADS_AT_ONCE + 1) if heads % n == 0)


def cost(tokens, keys, width, blocks):
    return pl.CostEstimate(
        flops=4 * tokens * keys * width * blocks,
        transcendentals=tokens * keys * (width // HD) * blocks,
        bytes_accessed=2 * width * (2 * tokens + 2 * keys * blocks),
    )


def attend_first(live, queries, blocks):
    tokens, width = queries.shape
    heads = heads_at_once(width // HD)
    chunk = pl.BlockSpec((tokens, heads * HD), lambda i: (0, i))
    return pl.pallas_call(
        functools.partial(first_kernel, len(blocks), heads),
        grid=(width // (heads * HD),),
        in_specs=[pl.BlockSpec(memory_space=pltpu.SMEM)] + [chunk] * (1 + 4 * len(blocks)),
        out_specs=[chunk, chunk],
        out_shape=[jax.ShapeDtypeStruct((tokens, width), jnp.float32)] * 2,
        scratch_shapes=[pltpu.VMEM((heads, tokens, HD), jnp.float32)] * 2,
        cost_estimate=cost(tokens, 2 * tokens, width, len(blocks)),
        name="attend_first",
    )(live, queries, *[a for block in blocks for a in block])


def attend_last(live, queries, blocks, before, stats):
    tokens, width = queries.shape
    heads = heads_at_once(width // HD)
    chunk = pl.BlockSpec((tokens, heads * HD), lambda i: (0, i))
    return pl.pallas_call(
        functools.partial(last_kernel, len(blocks), heads),
        grid=(width // (heads * HD),),
        in_specs=[pl.BlockSpec(memory_space=pltpu.SMEM)] + [chunk] * (3 + 4 * len(blocks)),
        out_specs=chunk,
        out_shape=jax.ShapeDtypeStruct((tokens, width), jnp.bfloat16),
        scratch_shapes=[pltpu.VMEM((heads, tokens, HD), jnp.float32)] * 2
        + [pltpu.VMEM((tokens, heads * HD), jnp.float32)],
        cost_estimate=cost(tokens, 2 * tokens, width, len(blocks)),
        name="attend_last",
    )(live, queries, *[a for block in blocks for a in block], before, stats)


def after(value, *others):
    return lax.optimization_barrier((value,) + others)[0]


def shards(phases, queries, keys, values, pattern):
    rows = lax.axis_size("row")
    cols = lax.axis_size("col")
    row = lax.axis_index("row")
    swap_pairs = [(c, cols - 1 - c) for c in range(cols)]

    def swapped(value):
        return lax.ppermute(value, "col", swap_pairs)

    def moved(value, phase):
        return lax.ppermute(value, "row", [(s, t) for s, (t, _) in sorted(phase.items())])

    flags = [jnp.ones((), jnp.int32)]
    own_row = lax.dynamic_index_in_dim(pattern, row, 0, keepdims=False)
    table = []
    for phase in phases:
        numbers = [len(OFFSETS)] * rows
        for to, number in phase.values():
            numbers[to] = number
        table.append(numbers)
    table = jnp.asarray(table, jnp.int32)[:, row]
    padded = jnp.concatenate([own_row, jnp.zeros((1,), jnp.int32)])
    arrived_live = jnp.sum(
        jnp.where(table[:, None] == jnp.arange(len(OFFSETS) + 1)[None, :], padded[None, :], 0), axis=1
    )

    x1, x2, near = phases[:3]
    k_x1 = moved(keys, x1)
    v_x1 = moved(values, x1)
    k_near = moved(keys, near)
    v_near = moved(values, near)
    k_own, v_own = swapped(keys), swapped(values)
    later = []
    for phase in [x2] + phases[3:]:
        later.append((moved(after(keys, k_x1), phase), moved(after(values, v_x1), phase)))

    def block(k, v):
        return (k, swapped(k), v, swapped(v))

    first = [(keys, k_own, values, v_own), block(k_near, v_near), block(k_x1, v_x1)]
    live_first = jnp.concatenate([jnp.ones((1,), jnp.int32), arrived_live[2:3], arrived_live[0:1]])
    before, stats = attend_first(live_first, queries, first)
    live_last = jnp.concatenate([arrived_live[1:2], arrived_live[3:]])
    return attend_last(live_last, queries, [block(k, v) for k, v in later], before, stats)


def solution(mesh):
    placed = P(("groups", "row", "col"), None)
    return jax.shard_map(
        functools.partial(shards, plan(mesh.shape["row"])),
        mesh=mesh,
        in_specs=(placed, placed, placed, P("groups", None)),
        out_specs=placed,
        check_vma=False,
    )
```

```python
import functools

import jax
import jax.numpy as jnp
from jax import lax
from jax.experimental import pallas as pl
from jax.experimental.pallas import tpu as pltpu
from jax.sharding import PartitionSpec as P


HD = 128
TILE_H = 4
OFFSETS = (0, -1, 1, -TILE_H, TILE_H)
SCALE = HD ** (-0.5) * 1.4426950408889634
FAR_BELOW = -1e30
HEADS_AT_ONCE = 4
VMEM_BYTES = 16 * 1024 * 1024


def plan(rows):
    edges = []
    for to in range(rows):
        for number, offset in enumerate(OFFSETS):
            source = to + offset
            if offset == 0 or not 0 <= source < rows:
                continue
            if abs(offset) == 1 and source // TILE_H != to // TILE_H:
                continue
            low = min(source, to)
            odd = (low // TILE_H) % 2
            late = low % TILE_H >= TILE_H // 2
            if abs(offset) == TILE_H:
                wanted = (0 if not late else 2) if not odd else None
            else:
                crossing = low % 2 == 1
                wanted = 1 if crossing == bool(odd) else 3
            edges.append((wanted is None, low, source, to, number, wanted))
    edges.sort()
    phases = [{}, {}, {}, {}]
    for _, _, source, to, number, wanted in edges:
        order = [] if wanted is None else [wanted]
        order += list(range(4, len(phases))) + [len(phases)]
        for index in order:
            if index == len(phases):
                phases.append({})
            phase = phases[index]
            if source not in phase and all(t != to for t, _ in phase.values()):
                phase[source] = (to, number)
                break
    return phases[:2] + phases[4:], phases[2:4]


def scores_of(q, keys, biases):
    scores = [
        lax.dot_general(q, k, (((1,), (1,)), ((), ())), preferred_element_type=jnp.float32) * SCALE
        for k in keys
    ]
    return [s if b is None else s + b for s, b in zip(scores, biases)]


def first_kernel(blocks, heads, bias_ref, q_ref, *refs):
    kv = refs[: 4 * blocks]
    out_ref, stat_ref = refs[4 * blocks :]
    for head in range(heads):
        here = slice(head * HD, (head + 1) * HD)
        keys, values, biases = [], [], []
        for number in range(blocks):
            k_own, k_other, v_own, v_other = kv[4 * number : 4 * number + 4]
            keys.append(jnp.concatenate([k_own[:, here], k_other[:, here]], axis=0))
            values += [v_own[:, here], v_other[:, here]]
            biases.append(None if number == 0 else bias_ref[number - 1])
        scores = jnp.concatenate(scores_of(q_ref[:, here], keys, biases), axis=1)
        top = jnp.max(scores, axis=1, keepdims=True)
        weights = jnp.exp2(scores - top)
        total = jnp.sum(weights, axis=1, keepdims=True)
        out = jnp.dot(
            weights.astype(jnp.bfloat16),
            jnp.concatenate(values, axis=0),
            preferred_element_type=jnp.float32,
        )
        out_ref[:, here] = out / total
        stat_ref[:, here] = jnp.broadcast_to(top + jnp.log2(total), out.shape)


def weigh_kernel(blocks, heads, bias_ref, q_ref, *refs):
    k_refs = refs[: 2 * blocks]
    before_ref, stat_ref = refs[2 * blocks : 2 * blocks + 2]
    weight_refs, base_ref = refs[2 * blocks + 2 : -1], refs[-1]
    keys_each = 2 * k_refs[0].shape[0]
    for head in range(heads):
        here = slice(head * HD, (head + 1) * HD)
        keys = [
            jnp.concatenate([k_refs[2 * n][:, here], k_refs[2 * n + 1][:, here]], axis=0)
            for n in range(blocks)
        ]
        biases = [bias_ref[n] for n in range(blocks)]
        scores = jnp.concatenate(scores_of(q_ref[:, here], keys, biases), axis=1)
        before = stat_ref[:, here][:, :1]
        top = jnp.maximum(before, jnp.max(scores, axis=1, keepdims=True))
        weights = jnp.exp2(scores - top)
        factor = jnp.exp2(before - top)
        inverse = 1.0 / (factor + jnp.sum(weights, axis=1, keepdims=True))
        weights = (weights * inverse).astype(jnp.bfloat16)
        for n in range(blocks):
            weight_refs[n][:, head * keys_each : (head + 1) * keys_each] = weights[
                :, n * keys_each : (n + 1) * keys_each
            ]
        base_ref[:, here] = before_ref[:, here] * (factor * inverse)


def last_kernel(blocks, heads, base_ref, *refs):
    weight_refs, v_refs, out_ref = refs[:blocks], refs[blocks : 3 * blocks], refs[-1]
    keys_each = 2 * v_refs[0].shape[0]
    for head in range(heads):
        here = slice(head * HD, (head + 1) * HD)
        weights = [w[:, head * keys_each : (head + 1) * keys_each] for w in weight_refs]
        out = jnp.dot(
            jnp.concatenate(weights, axis=1),
            jnp.concatenate([v[:, here] for v in v_refs], axis=0),
            preferred_element_type=jnp.float32,
        )
        out_ref[:, here] = (base_ref[:, here] + out).astype(out_ref.dtype)


def heads_at_once(heads):
    return max(n for n in range(1, HEADS_AT_ONCE + 1) if heads % n == 0)


def chunked(kernel, scalars, operands, out_types, blocks, dots):
    tokens, width = operands[0].shape
    heads = heads_at_once(width // HD)
    steps = width // (heads * HD)

    def spec(shape):
        return pl.BlockSpec((shape[0], shape[1] // steps), lambda i: (0, i))

    return pl.pallas_call(
        functools.partial(kernel, blocks, heads),
        grid=(steps,),
        in_specs=[pl.BlockSpec(memory_space=pltpu.SMEM)] * len(scalars)
        + [spec(a.shape) for a in operands],
        out_specs=[spec(t.shape) for t in out_types],
        out_shape=out_types,
        cost_estimate=pl.CostEstimate(
            flops=dots * 2 * tokens * 2 * tokens * width * blocks,
            transcendentals=tokens * 2 * tokens * (width // HD) * blocks,
            bytes_accessed=sum(a.size * a.dtype.itemsize for a in operands)
            + sum(t.size * t.dtype.itemsize for t in out_types),
        ),
        compiler_params=pltpu.CompilerParams(vmem_limit_bytes=VMEM_BYTES),
    )(*scalars, *operands)


def after(value, *others):
    return lax.optimization_barrier((value,) + others)[0]


def shards(stages, queries, keys, values, pattern):
    tokens, width = queries.shape
    rows = lax.axis_size("row")
    cols = lax.axis_size("col")
    row = lax.axis_index("row")

    def moved(value, phase):
        return lax.ppermute(value, "row", [(s, t) for s, (t, _) in sorted(phase.items())])

    def swapped(value, phase=None):
        reached = range(rows) if phase is None else sorted(t for t, _ in phase.values())
        pairs = [(r * cols + c, r * cols + cols - 1 - c) for r in reached for c in range(cols)]
        return lax.ppermute(value, ("row", "col"), pairs)

    def biases(stage):
        table = [[len(OFFSETS)] * len(stage) for _ in range(rows)]
        for index, phase in enumerate(stage):
            for to, number in phase.values():
                table[to][index] = number
        picks = jnp.asarray(table, jnp.int32)[row]
        here = jnp.arange(len(OFFSETS), dtype=jnp.int32)[None, :] == picks[:, None]
        live = jnp.sum(jnp.where(here, own_row, 0), axis=1)
        return jnp.where(live == 1, 0.0, FAR_BELOW).astype(jnp.float32)

    own_row = lax.dynamic_index_in_dim(pattern, row, 0, keepdims=True)
    early, late = stages
    k_early = [moved(keys, p) for p in early]
    v_early = [moved(values, p) for p in early]
    k_swap, v_swap = swapped(keys), swapped(values)
    k_again = after(keys, *k_early)
    v_again = after(values, *k_early)
    k_late = [moved(k_again, p) for p in late]
    v_late = [moved(v_again, p) for p in late]

    blocks = [keys, k_swap, values, v_swap]
    for k, v, p in zip(k_early, v_early, early):
        blocks += [k, swapped(k, p), v, swapped(v, p)]
    full = jax.ShapeDtypeStruct((tokens, width), jnp.float32)
    before, stats = chunked(
        first_kernel, [biases(early)], [queries] + blocks, [full] * 2, 1 + len(early), 2
    )
    k_both = []
    for k, p in zip(k_late, late):
        k_both += [k, swapped(k, p)]
    weight = jax.ShapeDtypeStruct((tokens, width // HD * 2 * tokens), jnp.bfloat16)
    *weights, base = chunked(
        weigh_kernel, [biases(late)], [queries] + k_both + [before, stats],
        [weight] * len(late) + [full], len(late), 1,
    )
    v_both = []
    for v, p in zip(v_late, late):
        v_both += [v, swapped(v, p)]
    out = jax.ShapeDtypeStruct((tokens, width), queries.dtype)
    return chunked(last_kernel, [], [base] + weights + v_both, [out], len(late), 1)[0]


def solution(mesh):
    placed = P(("groups", "row", "col"), None)
    stages = plan(mesh.shape["row"])

    def body(*args):
        return shards(stages, *args)

    return jax.shard_map(
        body,
        mesh=mesh,
        in_specs=(placed, placed, placed, P("groups", None)),
        out_specs=placed,
        check_vma=False,
    )
```

```python
import functools

import jax
import jax.numpy as jnp
from jax import lax
from jax.experimental import pallas as pl
from jax.experimental.pallas import tpu as pltpu
from jax.sharding import PartitionSpec as P


HD = 128
TILE_H = 4
OFFSETS = (0, -1, 1, -TILE_H, TILE_H)
SCALE = HD ** (-0.5) * 1.4426950408889634
FAR_BELOW = -1e30
HEADS_AT_ONCE = 4
VMEM_BYTES = 16 * 1024 * 1024


def plan(rows):
    edges = []
    for to in range(rows):
        for number, offset in enumerate(OFFSETS):
            source = to + offset
            if offset == 0 or not 0 <= source < rows:
                continue
            if abs(offset) == 1 and source // TILE_H != to // TILE_H:
                continue
            low = min(source, to)
            odd = (low // TILE_H) % 2
            late = low % TILE_H >= TILE_H // 2
            if abs(offset) == TILE_H:
                wanted = (0 if not late else 2) if not odd else None
            else:
                crossing = low % 2 == 1
                wanted = 1 if crossing == bool(odd) else 3
            edges.append((wanted is None, low, source, to, number, wanted))
    edges.sort()
    phases = [{}, {}, {}, {}]
    for _, _, source, to, number, wanted in edges:
        order = [] if wanted is None else [wanted]
        order += list(range(4, len(phases))) + [len(phases)]
        for index in order:
            if index == len(phases):
                phases.append({})
            phase = phases[index]
            if source not in phase and all(t != to for t, _ in phase.values()):
                phase[source] = (to, number)
                break
    return phases[:2] + phases[4:], phases[2:4]


def lanes(value):
    return [value[:, at : at + HD] for at in range(0, value.shape[1], HD)]


def over_row(reduce, join, slices):
    found = reduce(functools.reduce(join, slices), axis=1, keepdims=True)
    return jnp.broadcast_to(found, slices[0].shape)


def merge_kernel(blocks, heads, merging, finishing, *refs):
    refs = list(refs)
    bias_ref = refs.pop(0) if merging else None
    q_ref = refs.pop(0)
    k_refs, refs = refs[: 2 * blocks], refs[2 * blocks :]
    if finishing:
        v_refs, refs = refs[: 2 * blocks], refs[2 * blocks :]
    if merging:
        before_ref, stat_ref, *refs = refs
    if finishing:
        out_ref, total_ref, score_ref, weight_ref = refs
    else:
        weight_refs, base_ref, score_ref = refs[:blocks], refs[blocks], refs[blocks + 1]
    keys_each = 2 * k_refs[0].shape[0]
    kept = {}

    def score(head, here):
        for n in range(blocks):
            keys = jnp.concatenate([k_refs[2 * n][:, here], k_refs[2 * n + 1][:, here]], axis=0)
            found = lax.dot_general(
                q_ref[:, here], keys, (((1,), (1,)), ((), ())), preferred_element_type=jnp.float32
            )
            found = found * SCALE
            if merging:
                found = found + bias_ref[n]
            score_ref[head, :, n * keys_each : (n + 1) * keys_each] = found

    def weigh(head, here):
        slices = lanes(score_ref[head])
        top = over_row(jnp.max, jnp.maximum, slices)
        if merging:
            before = stat_ref[:, here]
            top = jnp.maximum(top, before)
        weights = [jnp.exp2(s - top) for s in slices]
        total = over_row(jnp.sum, jnp.add, weights)
        if merging:
            factor = jnp.exp2(before - top)
            total = total + factor
        inverse = 1.0 / total
        if finishing:
            total_ref[:, here] = top + jnp.log2(total)
            kept[head] = (inverse, factor * inverse if merging else None)
            for at, w in enumerate(weights):
                weight_ref[head, :, at * HD : (at + 1) * HD] = w.astype(jnp.bfloat16)
        else:
            base_ref[:, here] = before_ref[:, here] * (factor * inverse)
            each = keys_each // HD
            for at, w in enumerate(weights):
                start = head * keys_each + at % each * HD
                weight_refs[at // each][:, start : start + HD] = (w * inverse).astype(jnp.bfloat16)

    def mix(head, here):
        inverse, factor = kept.pop(head)
        out = jnp.dot(
            weight_ref[head],
            jnp.concatenate([v[:, here] for v in v_refs], axis=0),
            preferred_element_type=jnp.float32,
        )
        out = out * inverse
        if merging:
            out = out + before_ref[:, here] * factor
        out_ref[:, here] = out

    steps = [score, weigh, mix] if finishing else [score, weigh]
    for time in range(heads + len(steps) - 1):
        for number, step in enumerate(steps):
            head = time - number
            if 0 <= head < heads:
                step(head, slice(head * HD, (head + 1) * HD))


def last_kernel(blocks, heads, base_ref, *refs):
    weight_refs, v_refs, out_ref = refs[:blocks], refs[blocks : 3 * blocks], refs[-1]
    keys_each = 2 * v_refs[0].shape[0]
    for head in range(heads):
        here = slice(head * HD, (head + 1) * HD)
        weights = [w[:, head * keys_each : (head + 1) * keys_each] for w in weight_refs]
        out = jnp.dot(
            jnp.concatenate(weights, axis=1),
            jnp.concatenate([v[:, here] for v in v_refs], axis=0),
            preferred_element_type=jnp.float32,
        )
        out_ref[:, here] = (base_ref[:, here] + out).astype(out_ref.dtype)


def heads_at_once(heads):
    return max(n for n in range(1, HEADS_AT_ONCE + 1) if heads % n == 0)


def chunked(kernel, scalars, operands, out_types, blocks, dots, scratch=()):
    tokens, width = operands[0].shape
    heads = heads_at_once(width // HD)
    steps = width // (heads * HD)

    def spec(shape):
        return pl.BlockSpec((shape[0], shape[1] // steps), lambda i: (0, i))

    keys = 2 * tokens * blocks
    call = pl.pallas_call(
        functools.partial(kernel, blocks, heads),
        grid=(steps,),
        in_specs=[pl.BlockSpec(memory_space=pltpu.SMEM)] * len(scalars)
        + [spec(a.shape) for a in operands],
        out_specs=[spec(t.shape) for t in out_types],
        out_shape=out_types,
        scratch_shapes=[pltpu.VMEM((heads, tokens, keys), t) for t in scratch],
        cost_estimate=pl.CostEstimate(
            flops=dots * 2 * tokens * 2 * tokens * width * blocks,
            transcendentals=tokens * 2 * tokens * (width // HD) * blocks,
            bytes_accessed=sum(a.size * a.dtype.itemsize for a in operands)
            + sum(t.size * t.dtype.itemsize for t in out_types),
        ),
        compiler_params=pltpu.CompilerParams(vmem_limit_bytes=VMEM_BYTES),
    )
    return list(call(*scalars, *operands))


def after(value, *others):
    return lax.optimization_barrier((value,) + others)[0]


def shards(stages, queries, keys, values, pattern):
    tokens, width = queries.shape
    rows = lax.axis_size("row")
    cols = lax.axis_size("col")
    row = lax.axis_index("row")

    def moved(value, phase):
        return lax.ppermute(value, "row", [(s, t) for s, (t, _) in sorted(phase.items())])

    def swapped(value, phase=None):
        reached = range(rows) if phase is None else sorted(t for t, _ in phase.values())
        pairs = [(r * cols + c, r * cols + cols - 1 - c) for r in reached for c in range(cols)]
        return lax.ppermute(value, ("row", "col"), pairs)

    def biases(stage):
        table = [[len(OFFSETS)] * len(stage) for _ in range(rows)]
        for index, phase in enumerate(stage):
            for to, number in phase.values():
                table[to][index] = number
        picks = jnp.asarray(table, jnp.int32)[row]
        here = jnp.arange(len(OFFSETS), dtype=jnp.int32)[None, :] == picks[:, None]
        live = jnp.sum(jnp.where(here, own_row, 0), axis=1)
        return jnp.where(live == 1, 0.0, FAR_BELOW).astype(jnp.float32)

    own_row = lax.dynamic_index_in_dim(pattern, row, 0, keepdims=True)
    early, late = stages
    k_early = [moved(keys, p) for p in early]
    v_early = [moved(values, p) for p in early]
    k_swap, v_swap = swapped(keys), swapped(values)
    k_again = after(keys, *k_early)
    v_again = after(values, *v_early)
    k_late = [moved(k_again, p) for p in late]
    v_late = [moved(v_again, p) for p in late]

    full = jax.ShapeDtypeStruct((tokens, width), jnp.float32)

    def attend(merged, operands, blocks):
        def kernel(blocks, heads, *refs):
            merge_kernel(blocks, heads, merged is not None, True, *refs)

        scalars = [] if merged is None else [merged]
        scratch = (jnp.float32, jnp.bfloat16)
        return chunked(kernel, scalars, operands, [full] * 2, blocks, 2, scratch)

    def weigh(merged, operands, blocks):
        def kernel(blocks, heads, *refs):
            merge_kernel(blocks, heads, True, False, *refs)

        weight = jax.ShapeDtypeStruct((tokens, width // HD * 2 * tokens), jnp.bfloat16)
        outs = [weight] * blocks + [full]
        return chunked(kernel, [merged], operands, outs, blocks, 1, (jnp.float32,))

    carried = attend(None, [queries, keys, k_swap, values, v_swap], 1)
    k_both, v_both = [], []
    for k, v, p in zip(k_early, v_early, early):
        k_both += [k, swapped(k, p)]
        v_both += [v, swapped(v, p)]
    carried = attend(biases(early), [queries] + k_both + v_both + carried, len(early))
    k_both = []
    for k, p in zip(k_late, late):
        k_both += [k, swapped(k, p)]
    *weights, base = weigh(biases(late), [queries] + k_both + carried, len(late))
    v_both = []
    for v, p in zip(v_late, late):
        v_both += [v, swapped(v, p)]
    out = jax.ShapeDtypeStruct((tokens, width), queries.dtype)
    return chunked(last_kernel, [], [base] + weights + v_both, [out], len(late), 1)[0]


def solution(mesh):
    placed = P(("groups", "row", "col"), None)
    stages = plan(mesh.shape["row"])

    def body(*args):
        return shards(stages, *args)

    return jax.shard_map(
        body,
        mesh=mesh,
        in_specs=(placed, placed, placed, P("groups", None)),
        out_specs=placed,
        check_vma=False,
    )
```

```python
import functools

import jax
import jax.numpy as jnp
from jax import lax
from jax.experimental import pallas as pl
from jax.experimental.pallas import tpu as pltpu
from jax.sharding import PartitionSpec as P


HD = 128
TILE_H = 4
OFFSETS = (0, -1, 1, -TILE_H, TILE_H)
SCALE = HD ** (-0.5) * 1.4426950408889634
FAR_BELOW = -1e30
HEADS_AT_ONCE = 4
VMEM_BYTES = 16 * 1024 * 1024


def plan(rows):
    edges = []
    for to in range(rows):
        for number, offset in enumerate(OFFSETS):
            source = to + offset
            if offset == 0 or not 0 <= source < rows:
                continue
            if abs(offset) == 1 and source // TILE_H != to // TILE_H:
                continue
            low = min(source, to)
            odd = (low // TILE_H) % 2
            late = low % TILE_H >= TILE_H // 2
            if abs(offset) == TILE_H:
                wanted = (0 if not late else 2) if not odd else None
            else:
                crossing = low % 2 == 1
                wanted = 1 if crossing == bool(odd) else 3
            edges.append((wanted is None, low, source, to, number, wanted))
    edges.sort()
    phases = [{}, {}, {}, {}]
    for _, _, source, to, number, wanted in edges:
        order = [] if wanted is None else [wanted]
        order += list(range(4, len(phases))) + [len(phases)]
        for index in order:
            if index == len(phases):
                phases.append({})
            phase = phases[index]
            if source not in phase and all(t != to for t, _ in phase.values()):
                phase[source] = (to, number)
                break
    return phases[:2] + phases[4:], phases[2:4]


def lanes(value):
    return [value[:, at : at + HD] for at in range(0, value.shape[1], HD)]


def over_row(reduce, join, slices):
    found = reduce(functools.reduce(join, slices), axis=1, keepdims=True)
    return jnp.broadcast_to(found, slices[0].shape)


def merge_kernel(blocks, heads, merging, finishing, *refs):
    refs = list(refs)
    bias_ref = refs.pop(0) if merging else None
    q_ref = refs.pop(0)
    k_refs, refs = refs[: 2 * blocks], refs[2 * blocks :]
    if finishing:
        v_refs, refs = refs[: 2 * blocks], refs[2 * blocks :]
    if merging:
        before_ref, stat_ref, *refs = refs
    if finishing:
        out_ref, total_ref, score_ref, weight_ref = refs
    else:
        weight_refs, (base_ref, total_ref, score_ref) = refs[:blocks], refs[blocks:]
    keys_each = 2 * k_refs[0].shape[0]
    kept = {}

    def score(head, here):
        for n in range(blocks):
            keys = jnp.concatenate([k_refs[2 * n][:, here], k_refs[2 * n + 1][:, here]], axis=0)
            found = lax.dot_general(
                q_ref[:, here], keys, (((1,), (1,)), ((), ())), preferred_element_type=jnp.float32
            )
            found = found * SCALE
            if merging:
                found = found + bias_ref[n]
            score_ref[head, :, n * keys_each : (n + 1) * keys_each] = found

    def weigh(head, here):
        slices = lanes(score_ref[head])
        top = over_row(jnp.max, jnp.maximum, slices)
        if merging:
            before = stat_ref[:, here]
            top = jnp.maximum(top, before)
        weights = [jnp.exp2(s - top) for s in slices]
        total = over_row(jnp.sum, jnp.add, weights)
        if merging:
            factor = jnp.exp2(before - top)
            total = total + factor
        inverse = 1.0 / total
        total_ref[:, here] = top + jnp.log2(total)
        if finishing:
            kept[head] = (inverse, factor * inverse if merging else None)
            for at, w in enumerate(weights):
                weight_ref[head, :, at * HD : (at + 1) * HD] = w.astype(jnp.bfloat16)
        else:
            base_ref[:, here] = before_ref[:, here] * (factor * inverse)
            each = keys_each // HD
            for at, w in enumerate(weights):
                start = head * keys_each + at % each * HD
                weight_refs[at // each][:, start : start + HD] = (w * inverse).astype(jnp.bfloat16)

    def mix(head, here):
        inverse, factor = kept.pop(head)
        out = jnp.dot(
            weight_ref[head],
            jnp.concatenate([v[:, here] for v in v_refs], axis=0),
            preferred_element_type=jnp.float32,
        )
        out = out * inverse
        if merging:
            out = out + before_ref[:, here] * factor
        out_ref[:, here] = out

    steps = [score, weigh, mix] if finishing else [score, weigh]
    for time in range(heads + len(steps) - 1):
        for number, step in enumerate(steps):
            head = time - number
            if 0 <= head < heads:
                step(head, slice(head * HD, (head + 1) * HD))


def last_kernel(blocks, heads, base_ref, *refs):
    weight_refs, v_refs, out_ref = refs[:blocks], refs[blocks : 3 * blocks], refs[-1]
    keys_each = 2 * v_refs[0].shape[0]
    for head in range(heads):
        here = slice(head * HD, (head + 1) * HD)
        weights = [w[:, head * keys_each : (head + 1) * keys_each] for w in weight_refs]
        out = jnp.dot(
            jnp.concatenate(weights, axis=1),
            jnp.concatenate([v[:, here] for v in v_refs], axis=0),
            preferred_element_type=jnp.float32,
        )
        out_ref[:, here] = (base_ref[:, here] + out).astype(out_ref.dtype)


def heads_at_once(heads):
    return max(n for n in range(1, HEADS_AT_ONCE + 1) if heads % n == 0)


def chunked(kernel, scalars, operands, out_types, blocks, dots, scratch=(), vmem=None):
    tokens, width = operands[0].shape
    heads = heads_at_once(width // HD)
    steps = width // (heads * HD)

    def spec(shape):
        return pl.BlockSpec((shape[0], shape[1] // steps), lambda i: (0, i))

    keys = 2 * tokens * blocks
    call = pl.pallas_call(
        functools.partial(kernel, blocks, heads),
        grid=(steps,),
        in_specs=[pl.BlockSpec(memory_space=pltpu.SMEM)] * len(scalars)
        + [spec(a.shape) for a in operands],
        out_specs=[spec(t.shape) for t in out_types],
        out_shape=out_types,
        scratch_shapes=[pltpu.VMEM((heads, tokens, keys), t) for t in scratch],
        cost_estimate=pl.CostEstimate(
            flops=dots * 2 * tokens * 2 * tokens * width * blocks,
            transcendentals=tokens * 2 * tokens * (width // HD) * blocks,
            bytes_accessed=sum(a.size * a.dtype.itemsize for a in operands)
            + sum(t.size * t.dtype.itemsize for t in out_types),
        ),
        compiler_params=pltpu.CompilerParams(vmem_limit_bytes=vmem),
    )
    return list(call(*scalars, *operands))


def after(value, *others):
    return lax.optimization_barrier((value,) + others)[0]


def shards(stages, queries, keys, values, pattern):
    tokens, width = queries.shape
    rows = lax.axis_size("row")
    cols = lax.axis_size("col")
    row = lax.axis_index("row")

    def moved(value, phase):
        return lax.ppermute(value, "row", [(s, t) for s, (t, _) in sorted(phase.items())])

    def swapped(value, phase=None):
        reached = range(rows) if phase is None else sorted(t for t, _ in phase.values())
        pairs = [(r * cols + c, r * cols + cols - 1 - c) for r in reached for c in range(cols)]
        return lax.ppermute(value, ("row", "col"), pairs)

    def biases(stage):
        table = [[len(OFFSETS)] * len(stage) for _ in range(rows)]
        for index, phase in enumerate(stage):
            for to, number in phase.values():
                table[to][index] = number
        picks = jnp.asarray(table, jnp.int32)[row]
        here = jnp.arange(len(OFFSETS), dtype=jnp.int32)[None, :] == picks[:, None]
        live = jnp.sum(jnp.where(here, own_row, 0), axis=1)
        return jnp.where(live == 1, 0.0, FAR_BELOW).astype(jnp.float32)

    own_row = lax.dynamic_index_in_dim(pattern, row, 0, keepdims=True)
    early, late = stages
    k_early = [moved(keys, p) for p in early]
    v_early = [moved(values, p) for p in early]
    k_swap, v_swap = swapped(keys, None), swapped(values, None)
    k_again = after(keys, *k_early)
    v_again = after(values, *v_early)
    k_late = [moved(k_again, p) for p in late]
    v_late = [moved(v_again, p) for p in late]

    full = jax.ShapeDtypeStruct((tokens, width), jnp.float32)

    def attend(merged, operands, blocks):
        def kernel(blocks, heads, *refs):
            merge_kernel(blocks, heads, merged is not None, True, *refs)

        scalars = [] if merged is None else [merged]
        scratch = (jnp.float32, jnp.bfloat16)
        return chunked(kernel, scalars, operands, [full] * 2, blocks, 2, scratch)

    def weigh(merged, operands, blocks, vmem=None):
        def kernel(blocks, heads, *refs):
            merge_kernel(blocks, heads, True, False, *refs)

        weight = jax.ShapeDtypeStruct((tokens, width // HD * 2 * tokens), jnp.bfloat16)
        outs = [weight] * blocks + [full] * 2
        scratch = (jnp.float32,)
        *weights, base, stats = chunked(kernel, [merged], operands, outs, blocks, 1, scratch, vmem)
        return weights, base, stats

    def mix(base, weights, values, dtype, vmem=None):
        out = jax.ShapeDtypeStruct((tokens, width), dtype)
        return chunked(last_kernel, [], [base] + weights + values, [out], len(weights), 1, (), vmem)[0]

    def both(given, stage):
        found = []
        for value, phase in zip(given, stage):
            found += [value, swapped(value, phase)]
        return found

    before, stats = attend(None, [queries, keys, k_swap, values, v_swap], 1)
    k_both = both(k_early, early)
    weights, base, stats = weigh(biases(early), [queries] + k_both + [before, stats], len(early))
    v_both = both(v_early, early)
    before = mix(base, weights, v_both, jnp.float32)
    k_both = both(k_late, late)
    weights, base, _ = weigh(
        biases(late), [queries] + k_both + [before, stats], len(late), VMEM_BYTES
    )
    v_both = both(v_late, late)
    return mix(base, weights, v_both, queries.dtype, VMEM_BYTES)


def solution(mesh):
    placed = P(("groups", "row", "col"), None)
    stages = plan(mesh.shape["row"])

    def body(*args):
        return shards(stages, *args)

    return jax.shard_map(
        body,
        mesh=mesh,
        in_specs=(placed, placed, placed, P("groups", None)),
        out_specs=placed,
        check_vma=False,
    )
```

```python
import functools

import jax
import jax.numpy as jnp
from jax import lax
from jax.experimental import pallas as pl
from jax.experimental.pallas import tpu as pltpu
from jax.sharding import PartitionSpec as P


HD = 128
TILE_H = 4
OFFSETS = (0, -1, 1, -TILE_H, TILE_H)
SCALE = HD ** (-0.5) * 1.4426950408889634
FAR_BELOW = -1e30
HEADS_AT_ONCE = 4
VMEM_BYTES = 16 * 1024 * 1024


def plan(rows):
    near, relay, far = ({}, {}), ({}, {}), [({}, {}), ({}, {})]
    for row in range(rows):
        other = row ^ 1
        if other < rows:
            near[0][other] = row
            near[1][row] = OFFSETS.index(other - row)
        start = row - row % TILE_H
        if row % TILE_H in (1, 2) and start + TILE_H <= rows:
            other = 2 * start + 3 - row
            relay[0][other ^ 1] = row
            relay[1][row] = OFFSETS.index(other - row)
        for way in (0, 1):
            other = row + TILE_H if (row // TILE_H) % 2 == way else row - TILE_H
            if 0 <= other < rows:
                far[way][0][other] = row
                far[way][1][row] = OFFSETS.index(other - row)
    return near, relay, [pair for pair in far if pair[0]]


def lanes(value):
    return [value[:, at : at + HD] for at in range(0, value.shape[1], HD)]


def over_row(reduce, join, slices):
    found = reduce(functools.reduce(join, slices), axis=1, keepdims=True)
    return jnp.broadcast_to(found, slices[0].shape)


def attend_chunk(heads, merging, mixed, held, bias_ref, refs, score_ref, weight_ref):
    refs = list(refs)
    blocks = mixed + held
    q_ref = refs.pop(0)
    k_refs, refs = refs[: 2 * blocks], refs[2 * blocks :]
    v_refs, refs = refs[: 2 * mixed], refs[2 * mixed :]
    if merging:
        before_ref, stat_ref, *refs = refs
    out_ref, *refs = refs
    held_refs, refs = refs[:held], refs[held:]
    total_ref = refs[0] if refs else None
    keys_each = 2 * k_refs[0].shape[0]
    each = keys_each // HD
    kept = {}

    def score(head, here):
        for n in range(blocks):
            keys = jnp.concatenate([k_refs[2 * n][:, here], k_refs[2 * n + 1][:, here]], axis=0)
            found = lax.dot_general(
                q_ref[:, here], keys, (((1,), (1,)), ((), ())), preferred_element_type=jnp.float32
            )
            found = found * SCALE
            if merging:
                found = found + bias_ref[n]
            score_ref[head, :, n * keys_each : (n + 1) * keys_each] = found

    def weigh(head, here):
        slices = lanes(score_ref[head])
        top = over_row(jnp.max, jnp.maximum, slices)
        if merging:
            before = stat_ref[:, here]
            top = jnp.maximum(top, before)
        weights = [jnp.exp2(s - top) for s in slices]
        total = over_row(jnp.sum, jnp.add, weights)
        factor = None
        if merging:
            factor = jnp.exp2(before - top)
            total = total + factor
        inverse = 1.0 / total
        if total_ref is not None:
            total_ref[:, here] = top + jnp.log2(total)
        for at, w in enumerate(weights):
            n = at // each
            if n < mixed:
                weight_ref[head, :, at * HD : (at + 1) * HD] = w.astype(jnp.bfloat16)
            else:
                start = head * keys_each + at % each * HD
                held_refs[n - mixed][:, start : start + HD] = (w * inverse).astype(jnp.bfloat16)
        kept[head] = (inverse, factor * inverse if merging else None)

    def mix(head, here):
        inverse, factor = kept.pop(head)
        out = jnp.dot(
            weight_ref[head],
            jnp.concatenate([v[:, here] for v in v_refs], axis=0),
            preferred_element_type=jnp.float32,
        )
        out = out * inverse
        if merging:
            out = out + before_ref[:, here] * factor
        out_ref[:, here] = out

    steps = [score, weigh, mix]
    for time in range(heads + len(steps) - 1):
        for number, step in enumerate(steps):
            head = time - number
            if 0 <= head < heads:
                step(head, slice(head * HD, (head + 1) * HD))


def finish_chunk(heads, blocks, refs):
    base_ref, refs = refs[0], refs[1:]
    weight_refs, v_refs, out_ref = refs[:blocks], refs[blocks : 3 * blocks], refs[-1]
    keys_each = 2 * v_refs[0].shape[0]
    for head in range(heads):
        here = slice(head * HD, (head + 1) * HD)
        weights = [w[:, head * keys_each : (head + 1) * keys_each] for w in weight_refs]
        out = jnp.dot(
            jnp.concatenate(weights, axis=1),
            jnp.concatenate([v[:, here] for v in v_refs], axis=0),
            preferred_element_type=jnp.float32,
        )
        out_ref[:, here] = (base_ref[:, here] + out).astype(out_ref.dtype)


def divisor(heads, most):
    return max(n for n in range(1, most + 1) if heads % n == 0)


def call(chunk, at_once, scalars, operands, out_types, scratch, dots, keys):
    tokens, width = operands[0].shape
    heads = divisor(width // HD, at_once)
    steps = width // (heads * HD)
    arrays = len(operands) + len(out_types)

    def kernel(*refs):
        scalar_refs, refs = refs[: len(scalars)], refs[len(scalars) :]
        array_refs, scratch_refs = refs[:arrays], refs[arrays:]

        def step(i, carry):
            views = []
            for ref in array_refs:
                wide = ref.shape[1] // steps
                views.append(ref.at[:, pl.ds(pl.multiple_of(i * wide, wide), wide)])
            chunk(heads, scalar_refs, views, scratch_refs)
            return carry

        lax.fori_loop(0, steps, step, 0)

    whole = pl.BlockSpec(memory_space=pltpu.VMEM)
    run = pl.pallas_call(
        kernel,
        in_specs=[pl.BlockSpec(memory_space=pltpu.SMEM)] * len(scalars) + [whole] * len(operands),
        out_specs=[whole] * len(out_types),
        out_shape=out_types,
        scratch_shapes=[pltpu.VMEM((heads,) + shape, t) for shape, t in scratch],
        cost_estimate=pl.CostEstimate(
            flops=dots * 2 * tokens * keys * width,
            transcendentals=tokens * keys * (width // HD),
            bytes_accessed=sum(a.size * a.dtype.itemsize for a in list(operands) + list(out_types)),
        ),
        compiler_params=pltpu.CompilerParams(vmem_limit_bytes=VMEM_BYTES),
    )
    return list(run(*scalars, *operands))


def attend(bias, queries, k_pairs, v_pairs, before, more):
    tokens, width = queries.shape
    merging, mixed, held = before is not None, len(v_pairs), len(k_pairs) - len(v_pairs)
    keys = 2 * tokens * len(k_pairs)

    def chunk(heads, scalar_refs, views, scratch_refs):
        attend_chunk(heads, merging, mixed, held, *(scalar_refs or (None,)), views, *scratch_refs)

    full = jax.ShapeDtypeStruct((tokens, width), jnp.float32)
    weight = jax.ShapeDtypeStruct((tokens, 2 * tokens * (width // HD)), jnp.bfloat16)
    operands = [queries] + [a for p in k_pairs for a in p] + [a for p in v_pairs for a in p]
    operands += list(before) if merging else []
    outs = [full] + [weight] * held + ([full] if more else [])
    scratch = [((tokens, keys), jnp.float32), ((tokens, 2 * tokens * mixed), jnp.bfloat16)]
    scalars = [bias] if merging else []
    return call(chunk, HEADS_AT_ONCE, scalars, operands, outs, scratch, 2, keys)


def finish(base, weights, v_pairs, dtype):
    tokens, width = base.shape
    blocks = len(v_pairs)

    def chunk(heads, scalar_refs, views, scratch_refs):
        finish_chunk(heads, blocks, views)

    operands = [base] + weights + [a for p in v_pairs for a in p]
    outs = [jax.ShapeDtypeStruct((tokens, width), dtype)]
    return call(chunk, 10, [], operands, outs, [], 1, 2 * tokens * blocks)[0]


def after(value, *others):
    return lax.optimization_barrier((value,) + others)[0]


def shards(routes, queries, keys, values, pattern):
    rows = lax.axis_size("row")
    cols = lax.axis_size("col")
    row = lax.axis_index("row")
    near, relay, far = routes

    def moved(value, route):
        return lax.ppermute(value, "row", sorted(route[0].items()))

    def paired(value, route):
        reached = range(rows) if route is None else sorted(route[1])
        pairs = [(r * cols + c, r * cols + cols - 1 - c) for r in reached for c in range(cols)]
        return value, lax.ppermute(value, ("row", "col"), pairs)

    own_row = lax.dynamic_index_in_dim(pattern, row, 0, keepdims=True)

    def biases(*given):
        table = [[route[1].get(r, len(OFFSETS)) for route in given] for r in range(rows)]
        picks = jnp.asarray(table, jnp.int32)[row]
        here = jnp.arange(len(OFFSETS), dtype=jnp.int32)[None, :] == picks[:, None]
        live = jnp.sum(jnp.where(here, own_row, 0), axis=1)
        return jnp.where(live == 1, 0.0, FAR_BELOW).astype(jnp.float32)

    v_near = moved(values, near)
    k_far = [moved(keys, route) for route in far]
    v_far = [moved(values, route) for route in far]
    k_own, v_own = paired(keys, None), paired(values, None)
    k_near = moved(after(keys, v_near), near)
    v_relay = moved(v_near, relay)
    k_relay = moved(k_near, relay)

    carried = attend(None, queries, [k_own], [v_own], None, True)
    carried = attend(
        biases(near), queries, [paired(k_near, near)], [paired(v_near, near)], carried, True
    )
    k_pairs = [paired(k_relay, relay)]
    k_pairs += [paired(k, route) for k, route in zip(k_far, far)]
    base, *weights = attend(
        biases(relay, *far), queries, k_pairs, [paired(v_relay, relay)], carried, False
    )
    v_pairs = [paired(v, route) for v, route in zip(v_far, far)]
    return finish(base, weights, v_pairs, queries.dtype)


def solution(mesh):
    placed = P(("groups", "row", "col"), None)
    routes = plan(mesh.shape["row"])

    def body(*args):
        return shards(routes, *args)

    return jax.shard_map(
        body,
        mesh=mesh,
        in_specs=(placed, placed, placed, P("groups", None)),
        out_specs=placed,
        check_vma=False,
    )
```

```python
import functools

import jax
import jax.numpy as jnp
from jax import lax
from jax.experimental import pallas as pl
from jax.experimental.pallas import tpu as pltpu
from jax.sharding import PartitionSpec as P


HD = 128
TILE_H = 4
OFFSETS = (0, -1, 1, -TILE_H, TILE_H)
SCALE = HD ** (-0.5) * 1.4426950408889634
FAR_BELOW = -1e30
HEADS_AT_ONCE = 4
VMEM_BYTES = 16 * 1024 * 1024


def plan(rows):
    near, relay, cross = ({}, {}), ({}, {}), ({}, {})
    far = [({}, {}), ({}, {})]
    for row in range(rows):
        other = row ^ 1
        if other < rows:
            near[0][other] = row
            near[1][row] = OFFSETS.index(other - row)
        start = row - row % TILE_H
        if row % TILE_H in (1, 2) and start + TILE_H <= rows:
            other = 2 * start + 3 - row
            relay[0][other ^ 1] = row
            cross[0][other] = row
            relay[1][row] = cross[1][row] = OFFSETS.index(other - row)
        for way in (0, 1):
            other = row + TILE_H if (row // TILE_H) % 2 == way else row - TILE_H
            if 0 <= other < rows:
                far[way][0][other] = row
                far[way][1][row] = OFFSETS.index(other - row)
    return near, relay, cross, [pair for pair in far if pair[0]]


def lanes(value):
    return [value[:, at : at + HD] for at in range(0, value.shape[1], HD)]


def over_row(reduce, join, slices):
    found = reduce(functools.reduce(join, slices), axis=1, keepdims=True)
    return jnp.broadcast_to(found, slices[0].shape)


def attend_chunk(heads, merging, mixed, held, bias_ref, refs, score_ref, weight_ref):
    refs = list(refs)
    blocks = mixed + held
    q_ref = refs.pop(0)
    k_refs, refs = refs[: 2 * blocks], refs[2 * blocks :]
    v_refs, refs = refs[: 2 * mixed], refs[2 * mixed :]
    if merging:
        before_ref, stat_ref, *refs = refs
    out_ref, *refs = refs
    held_refs, refs = refs[:held], refs[held:]
    total_ref = refs[0] if refs else None
    keys_each = 2 * k_refs[0].shape[0]
    each = keys_each // HD
    kept = {}

    def score(head, here):
        for n in range(blocks):
            keys = jnp.concatenate([k_refs[2 * n][:, here], k_refs[2 * n + 1][:, here]], axis=0)
            found = lax.dot_general(
                q_ref[:, here], keys, (((1,), (1,)), ((), ())), preferred_element_type=jnp.float32
            )
            found = found * SCALE
            if merging:
                found = found + bias_ref[n]
            score_ref[head, :, n * keys_each : (n + 1) * keys_each] = found

    def weigh(head, here):
        slices = lanes(score_ref[head])
        top = over_row(jnp.max, jnp.maximum, slices)
        if merging:
            before = stat_ref[:, here]
            top = jnp.maximum(top, before)
        weights = [jnp.exp2(s - top) for s in slices]
        total = over_row(jnp.sum, jnp.add, weights)
        factor = None
        if merging:
            factor = jnp.exp2(before - top)
            total = total + factor
        inverse = 1.0 / total
        if total_ref is not None:
            total_ref[:, here] = top + jnp.log2(total)
        for at, w in enumerate(weights):
            n = at // each
            if n < mixed:
                weight_ref[head, :, at * HD : (at + 1) * HD] = w.astype(jnp.bfloat16)
            else:
                start = head * keys_each + at % each * HD
                held_refs[n - mixed][:, start : start + HD] = (w * inverse).astype(jnp.bfloat16)
        kept[head] = (inverse, factor * inverse if merging else None)

    def mix(head, here):
        inverse, factor = kept.pop(head)
        out = jnp.dot(
            weight_ref[head],
            jnp.concatenate([v[:, here] for v in v_refs], axis=0),
            preferred_element_type=jnp.float32,
        )
        out = out * inverse
        if merging:
            out = out + before_ref[:, here] * factor
        out_ref[:, here] = out

    steps = [score, weigh, mix]
    for time in range(heads + len(steps) - 1):
        for number, step in enumerate(steps):
            head = time - number
            if 0 <= head < heads:
                step(head, slice(head * HD, (head + 1) * HD))


def finish_chunk(heads, blocks, refs):
    base_ref, refs = refs[0], refs[1:]
    weight_refs, v_refs, out_ref = refs[:blocks], refs[blocks : 3 * blocks], refs[-1]
    keys_each = 2 * v_refs[0].shape[0]
    for head in range(heads):
        here = slice(head * HD, (head + 1) * HD)
        weights = [w[:, head * keys_each : (head + 1) * keys_each] for w in weight_refs]
        out = jnp.dot(
            jnp.concatenate(weights, axis=1),
            jnp.concatenate([v[:, here] for v in v_refs], axis=0),
            preferred_element_type=jnp.float32,
        )
        out_ref[:, here] = (base_ref[:, here] + out).astype(out_ref.dtype)


def divisor(heads, most):
    return max(n for n in range(1, most + 1) if heads % n == 0)


def call(chunk, at_once, scalars, operands, out_types, scratch, dots, keys):
    tokens, width = operands[0].shape
    heads = divisor(width // HD, at_once)
    steps = width // (heads * HD)
    arrays = len(operands) + len(out_types)

    def kernel(*refs):
        scalar_refs, refs = refs[: len(scalars)], refs[len(scalars) :]
        array_refs, scratch_refs = refs[:arrays], refs[arrays:]

        def step(i, carry):
            views = []
            for ref in array_refs:
                wide = ref.shape[1] // steps
                views.append(ref.at[:, pl.ds(pl.multiple_of(i * wide, wide), wide)])
            chunk(heads, scalar_refs, views, scratch_refs)
            return carry

        lax.fori_loop(0, steps, step, 0)

    whole = pl.BlockSpec(memory_space=pltpu.VMEM)
    run = pl.pallas_call(
        kernel,
        in_specs=[pl.BlockSpec(memory_space=pltpu.SMEM)] * len(scalars) + [whole] * len(operands),
        out_specs=[whole] * len(out_types),
        out_shape=out_types,
        scratch_shapes=[pltpu.VMEM((heads,) + shape, t) for shape, t in scratch],
        cost_estimate=pl.CostEstimate(
            flops=dots * 2 * tokens * keys * width,
            transcendentals=tokens * keys * (width // HD),
            bytes_accessed=sum(a.size * a.dtype.itemsize for a in list(operands) + list(out_types)),
        ),
        compiler_params=pltpu.CompilerParams(vmem_limit_bytes=VMEM_BYTES),
    )
    return list(run(*scalars, *operands))


def attend(bias, queries, k_pairs, v_pairs, before, more):
    tokens, width = queries.shape
    merging, mixed, held = before is not None, len(v_pairs), len(k_pairs) - len(v_pairs)
    keys = 2 * tokens * len(k_pairs)

    def chunk(heads, scalar_refs, views, scratch_refs):
        attend_chunk(heads, merging, mixed, held, *(scalar_refs or (None,)), views, *scratch_refs)

    full = jax.ShapeDtypeStruct((tokens, width), jnp.float32)
    weight = jax.ShapeDtypeStruct((tokens, 2 * tokens * (width // HD)), jnp.bfloat16)
    operands = [queries] + [a for p in k_pairs for a in p] + [a for p in v_pairs for a in p]
    operands += list(before) if merging else []
    outs = [full] + [weight] * held + ([full] if more else [])
    scratch = [((tokens, keys), jnp.float32), ((tokens, 2 * tokens * mixed), jnp.bfloat16)]
    scalars = [bias] if merging else []
    return call(chunk, HEADS_AT_ONCE, scalars, operands, outs, scratch, 2, keys)


def finish(base, weights, v_pairs, dtype):
    tokens, width = base.shape
    blocks = len(v_pairs)

    def chunk(heads, scalar_refs, views, scratch_refs):
        finish_chunk(heads, blocks, views)

    operands = [base] + weights + [a for p in v_pairs for a in p]
    outs = [jax.ShapeDtypeStruct((tokens, width), dtype)]
    return call(chunk, 10, [], operands, outs, [], 1, 2 * tokens * blocks)[0]


def after(value, *others):
    return lax.optimization_barrier((value,) + others)[0]


def shards(routes, queries, keys, values, pattern):
    rows = lax.axis_size("row")
    cols = lax.axis_size("col")
    row = lax.axis_index("row")
    near, relay, cross, far = routes

    def moved(value, route):
        return lax.ppermute(value, "row", sorted(route[0].items()))

    def paired(value, route):
        reached = range(rows) if route is None else sorted(route[1])
        pairs = [(r * cols + c, r * cols + cols - 1 - c) for r in reached for c in range(cols)]
        return value, lax.ppermute(value, ("row", "col"), pairs)

    own_row = lax.dynamic_index_in_dim(pattern, row, 0, keepdims=True)

    def biases(*given):
        table = [[route[1].get(r, len(OFFSETS)) for route in given] for r in range(rows)]
        picks = jnp.asarray(table, jnp.int32)[row]
        here = jnp.arange(len(OFFSETS), dtype=jnp.int32)[None, :] == picks[:, None]
        live = jnp.sum(jnp.where(here, own_row, 0), axis=1)
        return jnp.where(live == 1, 0.0, FAR_BELOW).astype(jnp.float32)

    v_near = moved(values, near)
    k_far = [moved(keys, route) for route in far]
    k_own, v_own = paired(keys, None), paired(values, None)
    k_near = moved(after(keys, v_near), near)
    v_relay = moved(v_near, relay)
    v_again = after(values, v_near)
    v_far = [moved(v_again, route) for route in far]
    k_cross = moved(after(keys, k_near), cross)

    carried = attend(None, queries, [k_own], [v_own], None, True)
    carried = attend(
        biases(near), queries, [paired(k_near, near)], [paired(v_near, near)], carried, True
    )
    k_pairs = [paired(k_cross, cross)]
    k_pairs += [paired(k, route) for k, route in zip(k_far, far)]
    base, *weights = attend(
        biases(relay, *far), queries, k_pairs, [paired(v_relay, relay)], carried, False
    )
    v_pairs = [paired(v, route) for v, route in zip(v_far, far)]
    return finish(base, weights, v_pairs, queries.dtype)


def solution(mesh):
    placed = P(("groups", "row", "col"), None)
    routes = plan(mesh.shape["row"])

    def body(*args):
        return shards(routes, *args)

    return jax.shard_map(
        body,
        mesh=mesh,
        in_specs=(placed, placed, placed, P("groups", None)),
        out_specs=placed,
        check_vma=False,
    )
```

```python
import functools

import jax
import jax.numpy as jnp
from jax import lax
from jax.experimental import pallas as pl
from jax.experimental.pallas import tpu as pltpu
from jax.sharding import PartitionSpec as P


HD = 128
TILE_H = 4
OFFSETS = (0, -1, 1, -TILE_H, TILE_H)
SCALE = HD ** (-0.5) * 1.4426950408889634
FAR_BELOW = -1e30
HEADS_AT_ONCE = 4
VMEM_BYTES = 16 * 1024 * 1024


def plan(rows):
    near, relay, cross = ({}, {}), ({}, {}), ({}, {})
    far = [({}, {}, {}), ({}, {}, {})]
    for row in range(rows):
        other = row ^ 1
        if other < rows:
            near[0][other] = row
            near[1][row] = OFFSETS.index(other - row)
        start = row - row % TILE_H
        if row % TILE_H in (1, 2) and start + TILE_H <= rows:
            other = 2 * start + 3 - row
            relay[0][other ^ 1] = row
            cross[0][other] = row
            relay[1][row] = cross[1][row] = OFFSETS.index(other - row)
        for way in (0, 1):
            other = row + TILE_H if (row // TILE_H) % 2 == way else row - TILE_H
            if 0 <= other < rows:
                far[way][0 if row % TILE_H >= TILE_H // 2 else 1][other] = row
                far[way][2][row] = OFFSETS.index(other - row)
    return near, relay, cross, [way for way in far if way[2]]


def lanes(value):
    return [value[:, at : at + HD] for at in range(0, value.shape[1], HD)]


def over_row(reduce, join, slices):
    found = reduce(functools.reduce(join, slices), axis=1, keepdims=True)
    return jnp.broadcast_to(found, slices[0].shape)


def take(refs, pairs):
    found, refs = [], list(refs)
    for pair in pairs:
        found.append([[refs.pop(0) for _ in half] for half in pair])
    return found, refs


def gathered(pair, here):
    return jnp.concatenate(
        [functools.reduce(jnp.add, [ref[:, here] for ref in half]) for half in pair], axis=0
    )


def attend_chunk(heads, merging, k_pairs, v_pairs, bias_ref, refs, score_ref, weight_ref):
    blocks, mixed = len(k_pairs), len(v_pairs)
    held = blocks - mixed
    q_ref, *refs = refs
    k_refs, refs = take(refs, k_pairs)
    v_refs, refs = take(refs, v_pairs)
    if merging:
        before_ref, stat_ref, *refs = refs
    out_ref, *refs = refs
    held_refs, refs = refs[:held], refs[held:]
    total_ref = refs[0] if refs else None
    keys_each = 2 * k_refs[0][0][0].shape[0]
    each = keys_each // HD
    kept = {}

    def score(head, here):
        for n in range(blocks):
            found = lax.dot_general(
                q_ref[:, here], gathered(k_refs[n], here), (((1,), (1,)), ((), ())), preferred_element_type=jnp.float32
            )
            found = found * SCALE
            if merging:
                found = found + bias_ref[n]
            score_ref[head, :, n * keys_each : (n + 1) * keys_each] = found

    def weigh(head, here):
        slices = lanes(score_ref[head])
        top = over_row(jnp.max, jnp.maximum, slices)
        if merging:
            before = stat_ref[:, here]
            top = jnp.maximum(top, before)
        weights = [jnp.exp2(s - top) for s in slices]
        total = over_row(jnp.sum, jnp.add, weights)
        factor = None
        if merging:
            factor = jnp.exp2(before - top)
            total = total + factor
        inverse = 1.0 / total
        if total_ref is not None:
            total_ref[:, here] = top + jnp.log2(total)
        for at, w in enumerate(weights):
            n = at // each
            if n < mixed:
                weight_ref[head, :, at * HD : (at + 1) * HD] = w.astype(jnp.bfloat16)
            else:
                start = head * keys_each + at % each * HD
                held_refs[n - mixed][:, start : start + HD] = (w * inverse).astype(jnp.bfloat16)
        kept[head] = (inverse, factor * inverse if merging else None)

    def mix(head, here):
        inverse, factor = kept.pop(head)
        out = jnp.dot(
            weight_ref[head],
            jnp.concatenate([gathered(pair, here) for pair in v_refs], axis=0),
            preferred_element_type=jnp.float32,
        )
        out = out * inverse
        if merging:
            out = out + before_ref[:, here] * factor
        out_ref[:, here] = out

    steps = [score, weigh, mix]
    for time in range(heads + len(steps) - 1):
        for number, step in enumerate(steps):
            head = time - number
            if 0 <= head < heads:
                step(head, slice(head * HD, (head + 1) * HD))


def finish_chunk(heads, v_pairs, refs):
    base_ref, *refs = refs
    weight_refs, refs = refs[: len(v_pairs)], refs[len(v_pairs) :]
    v_refs, (out_ref,) = take(refs, v_pairs)
    keys_each = 2 * v_refs[0][0][0].shape[0]
    for head in range(heads):
        here = slice(head * HD, (head + 1) * HD)
        weights = [w[:, head * keys_each : (head + 1) * keys_each] for w in weight_refs]
        out = jnp.dot(
            jnp.concatenate(weights, axis=1),
            jnp.concatenate([gathered(pair, here) for pair in v_refs], axis=0),
            preferred_element_type=jnp.float32,
        )
        out_ref[:, here] = (base_ref[:, here] + out).astype(out_ref.dtype)


def divisor(heads, most):
    return max(n for n in range(1, most + 1) if heads % n == 0)


def call(chunk, at_once, scalars, operands, out_types, scratch, dots, keys):
    tokens, width = operands[0].shape
    heads = divisor(width // HD, at_once)
    steps = width // (heads * HD)
    arrays = len(operands) + len(out_types)

    def kernel(*refs):
        scalar_refs, refs = refs[: len(scalars)], refs[len(scalars) :]
        array_refs, scratch_refs = refs[:arrays], refs[arrays:]

        def step(i, carry):
            views = []
            for ref in array_refs:
                wide = ref.shape[1] // steps
                views.append(ref.at[:, pl.ds(pl.multiple_of(i * wide, wide), wide)])
            chunk(heads, scalar_refs, views, scratch_refs)
            return carry

        lax.fori_loop(0, steps, step, 0)

    whole = pl.BlockSpec(memory_space=pltpu.VMEM)
    run = pl.pallas_call(
        kernel,
        in_specs=[pl.BlockSpec(memory_space=pltpu.SMEM)] * len(scalars) + [whole] * len(operands),
        out_specs=[whole] * len(out_types),
        out_shape=out_types,
        scratch_shapes=[pltpu.VMEM((heads,) + shape, t) for shape, t in scratch],
        cost_estimate=pl.CostEstimate(
            flops=dots * 2 * tokens * keys * width,
            transcendentals=tokens * keys * (width // HD),
            bytes_accessed=sum(a.size * a.dtype.itemsize for a in list(operands) + list(out_types)),
        ),
        compiler_params=pltpu.CompilerParams(vmem_limit_bytes=VMEM_BYTES),
    )
    return list(run(*scalars, *operands))


def attend(bias, queries, k_pairs, v_pairs, before, more):
    tokens, width = queries.shape
    merging, mixed, held = before is not None, len(v_pairs), len(k_pairs) - len(v_pairs)
    keys = 2 * tokens * len(k_pairs)

    def chunk(heads, scalar_refs, views, scratch_refs):
        bias = scalar_refs[0] if merging else None
        attend_chunk(heads, merging, k_pairs, v_pairs, bias, views, *scratch_refs)

    full = jax.ShapeDtypeStruct((tokens, width), jnp.float32)
    weight = jax.ShapeDtypeStruct((tokens, 2 * tokens * (width // HD)), jnp.bfloat16)
    operands = [queries] + [a for p in k_pairs + v_pairs for half in p for a in half]
    operands += list(before) if merging else []
    outs = [full] + [weight] * held + ([full] if more else [])
    scratch = [((tokens, keys), jnp.float32), ((tokens, 2 * tokens * mixed), jnp.bfloat16)]
    scalars = [bias] if merging else []
    return call(chunk, HEADS_AT_ONCE, scalars, operands, outs, scratch, 2, keys)


def finish(base, weights, v_pairs, dtype):
    tokens, width = base.shape
    blocks = len(v_pairs)

    def chunk(heads, scalar_refs, views, scratch_refs):
        finish_chunk(heads, v_pairs, views)

    operands = [base] + weights + [a for p in v_pairs for half in p for a in half]
    outs = [jax.ShapeDtypeStruct((tokens, width), dtype)]
    return call(chunk, 10, [], operands, outs, [], 1, 2 * tokens * blocks)[0]


def after(value, *others):
    return lax.optimization_barrier((value,) + others)[0]


def shards(routes, queries, keys, values, pattern):
    rows = lax.axis_size("row")
    cols = lax.axis_size("col")
    row = lax.axis_index("row")
    near, relay, cross, far = routes

    def moved(value, sends):
        return lax.ppermute(value, "row", sorted(sends.items()))

    def swapped(value, sends):
        reached = range(rows) if sends is None else sorted(sends.values())
        pairs = [(r * cols + c, r * cols + cols - 1 - c) for r in reached for c in range(cols)]
        return lax.ppermute(value, ("row", "col"), pairs)

    def paired(value, sends):
        return (value,), (swapped(value, sends),)

    own_row = lax.dynamic_index_in_dim(pattern, row, 0, keepdims=True)

    def biases(*given):
        table = [[route[-1].get(r, len(OFFSETS)) for route in given] for r in range(rows)]
        picks = jnp.asarray(table, jnp.int32)[row]
        here = jnp.arange(len(OFFSETS), dtype=jnp.int32)[None, :] == picks[:, None]
        live = jnp.sum(jnp.where(here, own_row, 0), axis=1)
        return jnp.where(live == 1, 0.0, FAR_BELOW).astype(jnp.float32)

    v_near = moved(values, near[0])
    k_soon = [moved(keys, way[0]) for way in far]
    v_soon = [moved(values, way[0]) for way in far]
    k_near = moved(keys, near[0])
    k_own, v_own = paired(keys, None), paired(values, None)
    k_again, v_again = after(keys, v_near), after(values, v_near)
    v_relay = moved(v_near, relay[0])
    k_cross = moved(k_again, cross[0])
    k_then = [moved(k_again, way[1]) for way in far]
    v_then = [moved(v_again, way[1]) for way in far]

    def joined(soon, then):
        found = []
        for n, way in enumerate(far):
            other_soon = swapped(soon[n], way[0])
            other_then = swapped(then[n], way[1])
            found.append(((soon[n], then[n]), (other_soon, other_then)))
        return found

    carried = attend(None, queries, [k_own], [v_own], None, True)
    carried = attend(
        biases(near), queries, [paired(k_near, near[0])], [paired(v_near, near[0])], carried, True
    )
    base, *weights = attend(
        biases(relay, *far),
        queries,
        [paired(k_cross, cross[0])] + joined(k_soon, k_then),
        [paired(v_relay, relay[0])],
        carried,
        False,
    )
    return finish(base, weights, joined(v_soon, v_then), queries.dtype)


def solution(mesh):
    placed = P(("groups", "row", "col"), None)
    routes = plan(mesh.shape["row"])

    def body(*args):
        return shards(routes, *args)

    return jax.shard_map(
        body,
        mesh=mesh,
        in_specs=(placed, placed, placed, P("groups", None)),
        out_specs=placed,
        check_vma=False,
    )
```

```python
import functools

import jax
import jax.numpy as jnp
from jax import lax
from jax.experimental import pallas as pl
from jax.experimental.pallas import tpu as pltpu
from jax.sharding import PartitionSpec as P


HD = 128
TILE_H = 4
OFFSETS = (0, -1, 1, -TILE_H, TILE_H)
SCALE = HD ** (-0.5) * 1.4426950408889634
FAR_BELOW = -1e30
HEADS_AT_ONCE = 4
VMEM_BYTES = 16 * 1024 * 1024


def plan(rows):
    near, cross = ({}, {}), ({}, {})
    far = [({}, {}), ({}, {})]
    for row in range(rows):
        other = row ^ 1
        if other < rows:
            near[0][other] = row
            near[1][row] = OFFSETS.index(other - row)
        start = row - row % TILE_H
        if row % TILE_H in (1, 2) and start + TILE_H <= rows:
            other = 2 * start + 3 - row
            cross[0][other] = row
            cross[1][row] = OFFSETS.index(other - row)
        for way in (0, 1):
            other = row + TILE_H if (row // TILE_H) % 2 == way else row - TILE_H
            if 0 <= other < rows:
                far[way][0][other] = row
                far[way][1][row] = OFFSETS.index(other - row)
    return [near, cross] + [pair for pair in far if pair[0]]


def lanes(value):
    return [value[:, at : at + HD] for at in range(0, value.shape[1], HD)]


def over_row(reduce, join, slices):
    found = reduce(functools.reduce(join, slices), axis=1, keepdims=True)
    return jnp.broadcast_to(found, slices[0].shape)


def attend_chunk(heads, merging, mixed, held, bias_ref, refs, score_ref, weight_ref=None):
    refs = list(refs)
    blocks = mixed + held
    q_ref = refs.pop(0)
    k_refs, refs = refs[: 2 * blocks], refs[2 * blocks :]
    v_refs, refs = refs[: 2 * mixed], refs[2 * mixed :]
    if merging:
        before_ref, stat_ref, *refs = refs
    out_ref, *refs = refs
    held_refs, refs = refs[:held], refs[held:]
    total_ref = refs[0] if refs else None
    keys_each = 2 * k_refs[0].shape[0]
    each = keys_each // HD
    kept = {}

    def score(head, here):
        for n in range(blocks):
            keys = jnp.concatenate([k_refs[2 * n][:, here], k_refs[2 * n + 1][:, here]], axis=0)
            found = lax.dot_general(
                q_ref[:, here], keys, (((1,), (1,)), ((), ())), preferred_element_type=jnp.float32
            )
            found = found * SCALE
            if merging:
                found = found + bias_ref[n]
            score_ref[head, :, n * keys_each : (n + 1) * keys_each] = found

    def weigh(head, here):
        slices = lanes(score_ref[head])
        top = over_row(jnp.max, jnp.maximum, slices)
        if merging:
            before = stat_ref[:, here]
            top = jnp.maximum(top, before)
        weights = [jnp.exp2(s - top) for s in slices]
        total = over_row(jnp.sum, jnp.add, weights)
        factor = None
        if merging:
            factor = jnp.exp2(before - top)
            total = total + factor
        inverse = 1.0 / total
        if total_ref is not None:
            total_ref[:, here] = top + jnp.log2(total)
        for at, w in enumerate(weights):
            n = at // each
            if n < mixed:
                weight_ref[head, :, at * HD : (at + 1) * HD] = w.astype(jnp.bfloat16)
            else:
                start = head * keys_each + at % each * HD
                held_refs[n - mixed][:, start : start + HD] = (w * inverse).astype(jnp.bfloat16)
        kept[head] = (inverse, factor * inverse if merging else None)

    def mix(head, here):
        inverse, factor = kept.pop(head)
        if not mixed:
            out_ref[:, here] = before_ref[:, here] * factor
            return
        out = jnp.dot(
            weight_ref[head],
            jnp.concatenate([v[:, here] for v in v_refs], axis=0),
            preferred_element_type=jnp.float32,
        )
        out = out * inverse
        if merging:
            out = out + before_ref[:, here] * factor
        out_ref[:, here] = out

    steps = [score, weigh, mix]
    for time in range(heads + len(steps) - 1):
        for number, step in enumerate(steps):
            head = time - number
            if 0 <= head < heads:
                step(head, slice(head * HD, (head + 1) * HD))


def finish_chunk(heads, blocks, refs):
    base_ref, refs = refs[0], refs[1:]
    weight_refs, v_refs, out_ref = refs[:blocks], refs[blocks : 3 * blocks], refs[-1]
    keys_each = 2 * v_refs[0].shape[0]
    for head in range(heads):
        here = slice(head * HD, (head + 1) * HD)
        weights = [w[:, head * keys_each : (head + 1) * keys_each] for w in weight_refs]
        out = jnp.dot(
            jnp.concatenate(weights, axis=1),
            jnp.concatenate([v[:, here] for v in v_refs], axis=0),
            preferred_element_type=jnp.float32,
        )
        out_ref[:, here] = (base_ref[:, here] + out).astype(out_ref.dtype)


def divisor(heads, most):
    return max(n for n in range(1, most + 1) if heads % n == 0)


def call(chunk, at_once, scalars, operands, out_types, scratch, dots, keys):
    tokens, width = operands[0].shape
    heads = divisor(width // HD, at_once)
    steps = width // (heads * HD)
    arrays = len(operands) + len(out_types)

    def kernel(*refs):
        scalar_refs, refs = refs[: len(scalars)], refs[len(scalars) :]
        array_refs, scratch_refs = refs[:arrays], refs[arrays:]

        def step(i, carry):
            views = []
            for ref in array_refs:
                wide = ref.shape[1] // steps
                views.append(ref.at[:, pl.ds(pl.multiple_of(i * wide, wide), wide)])
            chunk(heads, scalar_refs, views, scratch_refs)
            return carry

        lax.fori_loop(0, steps, step, 0)

    whole = pl.BlockSpec(memory_space=pltpu.VMEM)
    run = pl.pallas_call(
        kernel,
        in_specs=[pl.BlockSpec(memory_space=pltpu.SMEM)] * len(scalars) + [whole] * len(operands),
        out_specs=[whole] * len(out_types),
        out_shape=out_types,
        scratch_shapes=[pltpu.VMEM((heads,) + shape, t) for shape, t in scratch],
        cost_estimate=pl.CostEstimate(
            flops=dots * 2 * tokens * keys * width,
            transcendentals=tokens * keys * (width // HD),
            bytes_accessed=sum(a.size * a.dtype.itemsize for a in list(operands) + list(out_types)),
        ),
        compiler_params=pltpu.CompilerParams(vmem_limit_bytes=VMEM_BYTES),
    )
    return list(run(*scalars, *operands))


def attend(bias, queries, k_pairs, v_pairs, before, more):
    tokens, width = queries.shape
    merging, mixed, held = before is not None, len(v_pairs), len(k_pairs) - len(v_pairs)
    keys = 2 * tokens * len(k_pairs)

    def chunk(heads, scalar_refs, views, scratch_refs):
        attend_chunk(heads, merging, mixed, held, *(scalar_refs or (None,)), views, *scratch_refs)

    full = jax.ShapeDtypeStruct((tokens, width), jnp.float32)
    weight = jax.ShapeDtypeStruct((tokens, 2 * tokens * (width // HD)), jnp.bfloat16)
    operands = [queries] + [a for p in k_pairs for a in p] + [a for p in v_pairs for a in p]
    operands += list(before) if merging else []
    outs = [full] + [weight] * held + ([full] if more else [])
    scratch = [((tokens, keys), jnp.float32)]
    scratch += [((tokens, 2 * tokens * mixed), jnp.bfloat16)] if mixed else []
    scalars = [bias] if merging else []
    return call(chunk, HEADS_AT_ONCE, scalars, operands, outs, scratch, 2, keys)


def finish(base, weights, v_pairs, dtype):
    tokens, width = base.shape
    blocks = len(v_pairs)

    def chunk(heads, scalar_refs, views, scratch_refs):
        finish_chunk(heads, blocks, views)

    operands = [base] + weights + [a for p in v_pairs for a in p]
    outs = [jax.ShapeDtypeStruct((tokens, width), dtype)]
    return call(chunk, 10, [], operands, outs, [], 1, 2 * tokens * blocks)[0]


def shards(routes, queries, keys, values, pattern):
    rows = lax.axis_size("row")
    cols = lax.axis_size("col")
    row = lax.axis_index("row")

    def moved(value, route):
        return lax.ppermute(value, "row", sorted(route[0].items()))

    def paired(value, route):
        reached = range(rows) if route is None else sorted(route[1])
        pairs = [(r * cols + c, r * cols + cols - 1 - c) for r in reached for c in range(cols)]
        return value, lax.ppermute(value, ("row", "col"), pairs)

    own_row = lax.dynamic_index_in_dim(pattern, row, 0, keepdims=True)

    def biases(*given):
        table = [[route[1].get(r, len(OFFSETS)) for route in given] for r in range(rows)]
        picks = jnp.asarray(table, jnp.int32)[row]
        here = jnp.arange(len(OFFSETS), dtype=jnp.int32)[None, :] == picks[:, None]
        live = jnp.sum(jnp.where(here, own_row, 0), axis=1)
        return jnp.where(live == 1, 0.0, FAR_BELOW).astype(jnp.float32)

    ks = [moved(keys, route) for route in routes]
    vs = [moved(values, route) for route in routes]
    k_own, v_own = paired(keys, None), paired(values, None)
    carried = attend(None, queries, [k_own], [v_own], None, True)
    k_pairs = [paired(k, route) for k, route in zip(ks, routes)]
    base, *weights = attend(biases(*routes), queries, k_pairs, [], carried, False)
    v_pairs = [paired(v, route) for v, route in zip(vs, routes)]
    return finish(base, weights, v_pairs, queries.dtype)


def solution(mesh):
    placed = P(("groups", "row", "col"), None)
    routes = plan(mesh.shape["row"])

    def body(*args):
        return shards(routes, *args)

    return jax.shard_map(
        body,
        mesh=mesh,
        in_specs=(placed, placed, placed, P("groups", None)),
        out_specs=placed,
        check_vma=False,
    )
```

```python
import functools

import jax
import jax.numpy as jnp
from jax import lax
from jax.experimental import pallas as pl
from jax.experimental.pallas import tpu as pltpu
from jax.sharding import PartitionSpec as P


HD = 128
TILE_H = 4
OFFSETS = (0, -1, 1, -TILE_H, TILE_H)
SCALE = HD ** (-0.5) * 1.4426950408889634
FAR_BELOW = -1e30
HEADS_AT_ONCE = 4
PARTS = 2
VMEM_BYTES = 16 * 1024 * 1024


def plan(rows):
    near, back, cross, far = {}, {}, {}, [({}, {}), ({}, {})]
    visit, side = {}, {}
    for row in range(rows):
        other, start = row ^ 1, row - row % TILE_H
        if row % TILE_H in (1, 2):
            back[other] = row
            visit[row] = OFFSETS.index(other - row)
            other = 2 * start + TILE_H - 1 - row
            if other < rows:
                cross[other] = row
                side[row] = OFFSETS.index(other - row)
        elif other < rows:
            near[other] = row
            side[row] = OFFSETS.index(other - row)
        for way in (0, 1):
            other = row + TILE_H if (row // TILE_H) % 2 == way else row - TILE_H
            if 0 <= other < rows:
                far[way][0][other] = row
                far[way][1][row] = OFFSETS.index(other - row)
    return near, back, cross, [way for way in far if way[0]], visit, side


def lanes(value):
    return [value[:, at : at + HD] for at in range(0, value.shape[1], HD)]


def over_row(reduce, join, slices):
    found = reduce(functools.reduce(join, slices), axis=1, keepdims=True)
    return jnp.broadcast_to(found, slices[0].shape)


def gathered(pair, here):
    return jnp.concatenate(
        [functools.reduce(jnp.add, [ref[:, here] for ref in half]) for half in pair], axis=0
    )


def grouped(refs, pairs):
    refs = list(refs)
    return [[[refs.pop(0) for _ in half] for half in pair] for pair in pairs], refs


def flat(pairs):
    return [a for pair in pairs for half in pair for a in half]


def lane_of(stat_ref, lane):
    stats = stat_ref[...]
    at = lax.broadcasted_iota(jnp.int32, stats.shape, 1)
    found = jnp.sum(jnp.where(at == lane, stats, 0.0), axis=1, keepdims=True)
    return jnp.broadcast_to(found, stats.shape)


def attend_chunk(index, heads, k_pairs, visited, bias_ref, refs, score_ref, weight_ref):
    q_ref, *refs = refs
    k_refs, refs = grouped(refs, k_pairs)
    v_refs, refs = refs[:2], refs[2:]
    if visited:
        visit_ref, stat_ref, *refs = refs
    out_ref, *held_refs = refs
    keys_each = 2 * v_refs[0].shape[0]
    each = keys_each // HD
    kept = {}

    def score(head, here):
        for n, pair in enumerate(k_refs):
            found = lax.dot_general(
                q_ref[:, here],
                gathered(pair, here),
                (((1,), (1,)), ((), ())),
                preferred_element_type=jnp.float32,
            )
            found = found * SCALE
            if n > 0:
                found = found + bias_ref[n]
            score_ref[head, :, n * keys_each : (n + 1) * keys_each] = found

    def weigh(head, here):
        slices = lanes(score_ref[head])
        top = over_row(jnp.max, jnp.maximum, slices)
        if visited:
            before = lane_of(stat_ref, index * heads + head) + bias_ref[0]
            top = jnp.maximum(top, before)
        weights = [jnp.exp2(s - top) for s in slices]
        total = over_row(jnp.sum, jnp.add, weights)
        factor = None
        if visited:
            factor = jnp.exp2(before - top)
            total = total + factor
        inverse = 1.0 / total
        for at, w in enumerate(weights):
            n = at // each
            if n == 0:
                weight_ref[head, :, at * HD : (at + 1) * HD] = w.astype(jnp.bfloat16)
            else:
                start = head * keys_each + at % each * HD
                held_refs[n - 1][:, start : start + HD] = (w * inverse).astype(jnp.bfloat16)
        if not visited:
            at = lax.broadcasted_iota(jnp.int32, top.shape, 1)
            stats = held_refs[0]
            kept_stats = stats[...] if head > 0 else jnp.where(index == 0, 0.0, stats[...])
            stats[...] = jnp.where(at == index * heads + head, top + jnp.log2(total), kept_stats)
        kept[head] = (inverse, factor)

    def mix(head, here):
        inverse, factor = kept.pop(head)
        out = jnp.dot(
            weight_ref[head],
            jnp.concatenate([v[:, here] for v in v_refs], axis=0),
            preferred_element_type=jnp.float32,
        )
        if visited:
            out = out + factor * visit_ref[:, here].astype(jnp.float32)
        out_ref[:, here] = (out * inverse).astype(out_ref.dtype)

    steps = [score, weigh, mix]
    for time in range(heads + len(steps) - 1):
        for number, step in enumerate(steps):
            head = time - number
            if 0 <= head < heads:
                step(head, slice(head * HD, (head + 1) * HD))


def divisor(heads, most):
    return max(n for n in range(1, most + 1) if heads % n == 0)


def call(chunk, at_once, scalars, operands, out_types, scratch, dots, keys):
    tokens, width = operands[0].shape
    heads = divisor(width // HD, at_once)
    steps = width // (heads * HD)
    arrays = len(operands) + len(out_types)

    def kernel(*refs):
        scalar_refs, refs = refs[: len(scalars)], refs[len(scalars) :]
        array_refs, scratch_refs = refs[:arrays], refs[arrays:]

        def step(i, carry):
            views = []
            for ref in array_refs:
                wide = ref.shape[1] // steps
                whole = ref.shape[1] == HD
                at = pl.ds(pl.multiple_of(i * wide, wide), wide)
                views.append(ref if whole else ref.at[:, at])
            chunk(i, heads, scalar_refs, views, scratch_refs)
            return carry

        lax.fori_loop(0, steps, step, 0)

    whole = pl.BlockSpec(memory_space=pltpu.VMEM)
    run = pl.pallas_call(
        kernel,
        in_specs=[pl.BlockSpec(memory_space=pltpu.SMEM)] * len(scalars) + [whole] * len(operands),
        out_specs=[whole] * len(out_types),
        out_shape=out_types,
        scratch_shapes=[pltpu.VMEM((heads,) + shape, t) for shape, t in scratch],
        cost_estimate=cost(tokens, keys, width, dots),
        compiler_params=pltpu.CompilerParams(vmem_limit_bytes=VMEM_BYTES),
    )
    return list(run(*scalars, *operands))


def cost(tokens, keys, width, dots):
    return pl.CostEstimate(
        flops=dots * 2 * tokens * keys * width,
        transcendentals=tokens * keys * (width // HD),
        bytes_accessed=2 * width * (2 * tokens + dots * keys),
    )


def attend(bias, queries, k_pairs, v_own, visit):
    tokens, width = queries.shape
    held, visited = len(k_pairs) - 1, visit is not None
    keys = 2 * tokens * len(k_pairs)

    def chunk(index, heads, scalar_refs, views, scratch_refs):
        bias_ref = scalar_refs[0] if visited else None
        attend_chunk(index, heads, k_pairs, visited, bias_ref, views, *scratch_refs)

    full = jax.ShapeDtypeStruct((tokens, width), jnp.float32 if visited else jnp.bfloat16)
    weight = jax.ShapeDtypeStruct((tokens, 2 * tokens * (width // HD)), jnp.bfloat16)
    outs = [full] + [weight] * held
    outs += [] if visited else [jax.ShapeDtypeStruct((tokens, HD), jnp.float32)]
    operands = [queries] + flat(k_pairs) + flat([v_own]) + (list(visit) if visited else [])
    scratch = [((tokens, keys), jnp.float32), ((tokens, 2 * tokens), jnp.bfloat16)]
    scalars = [bias] if visited else []
    return call(chunk, HEADS_AT_ONCE, scalars, operands, outs, scratch, 2, keys)


def mix(base, weights, v_pair):
    tokens = base.shape[0]

    def chunk(index, heads, scalar_refs, views, scratch_refs):
        base_ref, weight_ref, *v_refs, out_ref = views
        pair = grouped(v_refs, [v_pair])[0][0]
        for head in range(heads):
            here = slice(head * HD, (head + 1) * HD)
            out_ref[:, here] = base_ref[:, here] + jnp.dot(
                weight_ref[:, head * 2 * tokens : (head + 1) * 2 * tokens],
                gathered(pair, here),
                preferred_element_type=jnp.float32,
            )

    outs = [jax.ShapeDtypeStruct(base.shape, base.dtype)]
    operands = [base, weights] + flat([v_pair])
    return call(chunk, 10, [], operands, outs, [], 1, 2 * tokens)[0]


def finish(part, parts, base, weights, v_pairs, dtype, so_far):
    tokens, width = base.shape
    blocks, heads = len(v_pairs), width // HD // parts
    at_once = divisor(heads, 5)
    started, cols = part * heads * HD, heads * HD

    def kernel(base_ref, *refs):
        weight_refs, refs = refs[:blocks], refs[blocks:]
        v_refs, refs = refs[: 2 * blocks], refs[2 * blocks :]
        out_ref, held_ref, sems = refs[-3:]
        keys_each = 2 * tokens
        copies = []
        for step in range(heads // at_once):
            for head in range(step * at_once, (step + 1) * at_once):
                here = slice(head * HD, (head + 1) * HD)
                there = slice(started + head * HD, started + (head + 1) * HD)
                first = (part * heads + head) * keys_each
                chosen = [v[:, here] for v in v_refs]
                out = jnp.dot(
                    jnp.concatenate([w[:, first : first + keys_each] for w in weight_refs], axis=1),
                    jnp.concatenate(chosen, axis=0),
                    preferred_element_type=jnp.float32,
                )
                held_ref[:, here] = (base_ref[:, there] + out).astype(held_ref.dtype)
            wide = at_once * HD
            copies.append(
                pltpu.make_async_copy(
                    held_ref.at[:, pl.ds(step * wide, wide)],
                    out_ref.at[:, pl.ds(started + step * wide, wide)],
                    sems.at[step],
                )
            )
            copies[-1].start()
        for copy in copies:
            copy.wait()

    whole, anywhere = pl.BlockSpec(memory_space=pltpu.VMEM), pl.BlockSpec(memory_space=pl.ANY)
    operands = [base] + weights + flat(v_pairs)
    aliases = {} if so_far is None else {len(operands): 0}
    return pl.pallas_call(
        kernel,
        in_specs=[whole] * len(operands) + [anywhere] * len(aliases),
        out_specs=anywhere,
        out_shape=jax.ShapeDtypeStruct((tokens, width), dtype),
        scratch_shapes=[
            pltpu.VMEM((tokens, cols), dtype),
            pltpu.SemaphoreType.DMA((heads // at_once,)),
        ],
        input_output_aliases=aliases,
        cost_estimate=cost(tokens, 2 * tokens * blocks, cols, 1),
        compiler_params=pltpu.CompilerParams(vmem_limit_bytes=VMEM_BYTES),
    )(*operands, *([] if so_far is None else [so_far]))


def shards(routes, queries, keys, values, pattern):
    rows = lax.axis_size("row")
    cols = lax.axis_size("col")
    row = lax.axis_index("row")
    near, back, cross, far, visit, side = routes

    def moved(value, sends):
        return lax.ppermute(value, "row", sorted(sends.items()))

    def swapped(value, sends):
        reached = range(rows) if sends is None else sorted(sends.values())
        pairs = [(r * cols + c, r * cols + cols - 1 - c) for r in reached for c in range(cols)]
        return lax.ppermute(value, ("row", "col"), pairs)

    def paired(value, sends):
        return (value,), (swapped(value, sends),)

    def joined(of_near, of_cross):
        first = paired(of_near, near)
        second = paired(of_cross, cross)
        return tuple(a + b for a, b in zip(first, second))

    own_row = lax.dynamic_index_in_dim(pattern, row, 0, keepdims=True)

    def biases(*candidates):
        table = [[given.get(r, len(OFFSETS)) for given in candidates] for r in range(rows)]
        picks = jnp.asarray(table, jnp.int32)[row]
        here = jnp.arange(len(OFFSETS), dtype=jnp.int32)[None, :] == picks[:, None]
        live = jnp.sum(jnp.where(here, own_row, 0), axis=1)
        return jnp.where(live == 1, 0.0, FAR_BELOW).astype(jnp.float32)

    cut = values.shape[1] // PARTS
    visitors = moved(queries, near)
    k_far = [moved(keys, way[0]) for way in far]
    k_cross = moved(keys, cross)
    k_near = moved(keys, near)
    v_cross = moved(values, cross)
    v_near = moved(values, near)
    k_own, v_own = paired(keys, None), paired(values, None)

    result, stats = attend(None, visitors, [k_own], v_own, None)
    visited = (moved(result, back), moved(stats, back))

    k_pairs = [k_own, joined(k_near, k_cross)]
    k_pairs += [paired(k, way[0]) for k, way in zip(k_far, far)]
    bias = biases(visit, side, *[way[1] for way in far])
    base, of_side, *weights = attend(bias, queries, k_pairs, v_own, visited)
    base = mix(base, of_side, joined(v_near, v_cross))
    out = None
    for part in range(PARTS):
        here = values[:, part * cut : (part + 1) * cut]
        v_pairs = []
        for way in far:
            v = moved(here, way[0])
            v_pairs.append(paired(v, way[0]))
        out = finish(part, PARTS, base, weights, v_pairs, queries.dtype, out)
    return out


def solution(mesh):
    placed = P(("groups", "row", "col"), None)
    routes = plan(mesh.shape["row"])

    def body(*args):
        return shards(routes, *args)

    return jax.shard_map(
        body,
        mesh=mesh,
        in_specs=(placed, placed, placed, P("groups", None)),
        out_specs=placed,
        check_vma=False,
    )
```

```python
import functools

import jax
import jax.numpy as jnp
from jax import lax
from jax.experimental import pallas as pl
from jax.experimental.pallas import tpu as pltpu
from jax.sharding import PartitionSpec as P


HD = 128
TILE_H = 4
OFFSETS = (0, -1, 1, -TILE_H, TILE_H)
SCALE = HD ** (-0.5) * 1.4426950408889634
FAR_BELOW = -1e30
HEADS_AT_ONCE = 4
PARTS = 2
VMEM_BYTES = 16 * 1024 * 1024


def plan(rows):
    near, back, cross, far = {}, {}, {}, [({}, {}), ({}, {})]
    visit, side = {}, {}
    for row in range(rows):
        other, start = row ^ 1, row - row % TILE_H
        if row % TILE_H in (1, 2):
            back[other] = row
            visit[row] = OFFSETS.index(other - row)
            other = 2 * start + TILE_H - 1 - row
            if other < rows:
                cross[other] = row
                side[row] = OFFSETS.index(other - row)
        elif other < rows:
            near[other] = row
            side[row] = OFFSETS.index(other - row)
        for way in (0, 1):
            other = row + TILE_H if (row // TILE_H) % 2 == way else row - TILE_H
            if 0 <= other < rows:
                far[way][0][other] = row
                far[way][1][row] = OFFSETS.index(other - row)
    return near, back, cross, [way for way in far if way[0]], visit, side


def lanes(value):
    return [value[:, at : at + HD] for at in range(0, value.shape[1], HD)]


def over_row(reduce, join, slices):
    found = reduce(functools.reduce(join, slices), axis=1, keepdims=True)
    return jnp.broadcast_to(found, slices[0].shape)


def gathered(pair, here):
    return jnp.concatenate(
        [functools.reduce(jnp.add, [ref[:, here] for ref in half]) for half in pair], axis=0
    )


def grouped(refs, pairs):
    refs = list(refs)
    return [[[refs.pop(0) for _ in half] for half in pair] for pair in pairs], refs


def flat(pairs):
    return [a for pair in pairs for half in pair for a in half]


def lane_of(stat_ref, lane):
    stats = stat_ref[...]
    at = lax.broadcasted_iota(jnp.int32, stats.shape, 1)
    found = jnp.sum(jnp.where(at == lane, stats, 0.0), axis=1, keepdims=True)
    return jnp.broadcast_to(found, stats.shape)


def attend_chunk(index, heads, k_pairs, bias_ref, refs, score_ref, weight_ref):
    q_ref, *refs = refs
    k_refs, refs = grouped(refs, k_pairs)
    v_refs, refs = refs[:2], refs[2:]
    out_ref, *held_refs, stat_ref = refs
    keys_each = 2 * v_refs[0].shape[0]
    each = keys_each // HD
    kept = {}

    def score(head, here):
        for n, pair in enumerate(k_refs):
            found = lax.dot_general(
                q_ref[:, here],
                gathered(pair, here),
                (((1,), (1,)), ((), ())),
                preferred_element_type=jnp.float32,
            )
            found = found * SCALE
            if n > 0:
                found = found + bias_ref[n - 1]
            score_ref[head, :, n * keys_each : (n + 1) * keys_each] = found

    def weigh(head, here):
        slices = lanes(score_ref[head])
        top = over_row(jnp.max, jnp.maximum, slices)
        weights = [jnp.exp2(s - top) for s in slices]
        total = over_row(jnp.sum, jnp.add, weights)
        inverse = 1.0 / total
        for at, w in enumerate(weights):
            n = at // each
            if n == 0:
                weight_ref[head, :, at * HD : (at + 1) * HD] = w.astype(jnp.bfloat16)
            else:
                start = head * keys_each + at % each * HD
                held_refs[n - 1][:, start : start + HD] = (w * inverse).astype(jnp.bfloat16)
        at = lax.broadcasted_iota(jnp.int32, top.shape, 1)
        stats = stat_ref[...] if head > 0 else jnp.where(index == 0, 0.0, stat_ref[...])
        stat_ref[...] = jnp.where(at == index * heads + head, top + jnp.log2(total), stats)
        kept[head] = inverse

    def mix(head, here):
        out = jnp.dot(
            weight_ref[head],
            jnp.concatenate([v[:, here] for v in v_refs], axis=0),
            preferred_element_type=jnp.float32,
        )
        out_ref[:, here] = (out * kept.pop(head)).astype(out_ref.dtype)

    steps = [score, weigh, mix]
    for time in range(heads + len(steps) - 1):
        for number, step in enumerate(steps):
            head = time - number
            if 0 <= head < heads:
                step(head, slice(head * HD, (head + 1) * HD))


def divisor(heads, most):
    return max(n for n in range(1, most + 1) if heads % n == 0)


def call(chunk, at_once, scalars, operands, out_types, scratch, dots, keys):
    tokens, width = operands[0].shape
    heads = divisor(width // HD, at_once)
    steps = width // (heads * HD)
    arrays = len(operands) + len(out_types)

    def kernel(*refs):
        scalar_refs, refs = refs[: len(scalars)], refs[len(scalars) :]
        array_refs, scratch_refs = refs[:arrays], refs[arrays:]

        def step(i, carry):
            views = []
            for ref in array_refs:
                wide = ref.shape[1] // steps
                whole = ref.shape[1] == HD
                at = pl.ds(pl.multiple_of(i * wide, wide), wide)
                views.append(ref if whole else ref.at[:, at])
            chunk(i, heads, scalar_refs, views, scratch_refs)
            return carry

        lax.fori_loop(0, steps, step, 0)

    whole = pl.BlockSpec(memory_space=pltpu.VMEM)
    run = pl.pallas_call(
        kernel,
        in_specs=[pl.BlockSpec(memory_space=pltpu.SMEM)] * len(scalars) + [whole] * len(operands),
        out_specs=[whole] * len(out_types),
        out_shape=out_types,
        scratch_shapes=[pltpu.VMEM((heads,) + shape, t) for shape, t in scratch],
        cost_estimate=cost(tokens, keys, width, dots),
        compiler_params=pltpu.CompilerParams(vmem_limit_bytes=VMEM_BYTES),
    )
    return list(run(*scalars, *operands))


def cost(tokens, keys, width, dots):
    return pl.CostEstimate(
        flops=dots * 2 * tokens * keys * width,
        transcendentals=tokens * keys * (width // HD),
        bytes_accessed=2 * width * (2 * tokens + dots * keys),
    )


def attend(bias, queries, k_pairs, v_own, dtype):
    tokens, width = queries.shape
    held = len(k_pairs) - 1
    keys = 2 * tokens * len(k_pairs)

    def chunk(index, heads, scalar_refs, views, scratch_refs):
        bias_ref = scalar_refs[0] if held else None
        attend_chunk(index, heads, k_pairs, bias_ref, views, *scratch_refs)

    weight = jax.ShapeDtypeStruct((tokens, 2 * tokens * (width // HD)), jnp.bfloat16)
    outs = [jax.ShapeDtypeStruct((tokens, width), dtype)] + [weight] * held
    outs += [jax.ShapeDtypeStruct((tokens, HD), jnp.float32)]
    operands = [queries] + flat(k_pairs) + flat([v_own])
    scratch = [((tokens, keys), jnp.float32), ((tokens, 2 * tokens), jnp.bfloat16)]
    scalars = [bias] if held else []
    return call(chunk, HEADS_AT_ONCE, scalars, operands, outs, scratch, 2, keys)


def mix(bias, base, weights, v_pair, stats, visit, visit_stats):
    tokens = base.shape[0]

    def chunk(index, heads, scalar_refs, views, scratch_refs):
        base_ref, weight_ref, *refs = views
        (pair,), refs = grouped(refs, [v_pair])
        stat_ref, visit_ref, visit_stat_ref, out_ref, share_ref = refs
        for head in range(heads):
            here = slice(head * HD, (head + 1) * HD)
            out = base_ref[:, here] + jnp.dot(
                weight_ref[:, head * 2 * tokens : (head + 1) * 2 * tokens],
                gathered(pair, here),
                preferred_element_type=jnp.float32,
            )
            mine = lane_of(stat_ref, index * heads + head)
            theirs = lane_of(visit_stat_ref, index * heads + head) + scalar_refs[0][0]
            top = jnp.maximum(mine, theirs)
            mine, theirs = jnp.exp2(mine - top), jnp.exp2(theirs - top)
            inverse = 1.0 / (mine + theirs)
            share = mine * inverse
            share_ref[:, here] = share
            out_ref[:, here] = share * out + (theirs * inverse) * visit_ref[:, here].astype(jnp.float32)

    outs = [jax.ShapeDtypeStruct(base.shape, base.dtype)] * 2
    operands = [base, weights] + flat([v_pair]) + [stats, visit, visit_stats]
    return call(chunk, 10, [bias], operands, outs, [], 1, 2 * tokens)


def finish(part, parts, base, share, weights, v_pairs, dtype, so_far):
    tokens, width = base.shape
    blocks, heads = len(v_pairs), width // HD // parts
    at_once = divisor(heads, 5)
    started, cols = part * heads * HD, heads * HD

    def kernel(base_ref, share_ref, *refs):
        weight_refs, refs = refs[:blocks], refs[blocks:]
        v_refs, refs = refs[: 2 * blocks], refs[2 * blocks :]
        out_ref, held_ref, sems = refs[-3:]
        keys_each = 2 * tokens
        copies = []
        for step in range(heads // at_once):
            for head in range(step * at_once, (step + 1) * at_once):
                here = slice(head * HD, (head + 1) * HD)
                there = slice(started + head * HD, started + (head + 1) * HD)
                first = (part * heads + head) * keys_each
                chosen = [v[:, here] for v in v_refs]
                out = jnp.dot(
                    jnp.concatenate([w[:, first : first + keys_each] for w in weight_refs], axis=1),
                    jnp.concatenate(chosen, axis=0),
                    preferred_element_type=jnp.float32,
                )
                held_ref[:, here] = (base_ref[:, there] + share_ref[:, there] * out).astype(held_ref.dtype)
            wide = at_once * HD
            copies.append(
                pltpu.make_async_copy(
                    held_ref.at[:, pl.ds(step * wide, wide)],
                    out_ref.at[:, pl.ds(started + step * wide, wide)],
                    sems.at[step],
                )
            )
            copies[-1].start()
        for copy in copies:
            copy.wait()

    whole, anywhere = pl.BlockSpec(memory_space=pltpu.VMEM), pl.BlockSpec(memory_space=pl.ANY)
    operands = [base, share] + weights + flat(v_pairs)
    aliases = {} if so_far is None else {len(operands): 0}
    return pl.pallas_call(
        kernel,
        in_specs=[whole] * len(operands) + [anywhere] * len(aliases),
        out_specs=anywhere,
        out_shape=jax.ShapeDtypeStruct((tokens, width), dtype),
        scratch_shapes=[
            pltpu.VMEM((tokens, cols), dtype),
            pltpu.SemaphoreType.DMA((heads // at_once,)),
        ],
        input_output_aliases=aliases,
        cost_estimate=cost(tokens, 2 * tokens * blocks, cols, 1),
        compiler_params=pltpu.CompilerParams(vmem_limit_bytes=VMEM_BYTES),
    )(*operands, *([] if so_far is None else [so_far]))


def shards(routes, queries, keys, values, pattern):
    rows = lax.axis_size("row")
    cols = lax.axis_size("col")
    row = lax.axis_index("row")
    near, back, cross, far, visit, side = routes

    def moved(value, sends):
        return lax.ppermute(value, "row", sorted(sends.items()))

    def swapped(value, sends):
        reached = range(rows) if sends is None else sorted(sends.values())
        pairs = [(r * cols + c, r * cols + cols - 1 - c) for r in reached for c in range(cols)]
        return lax.ppermute(value, ("row", "col"), pairs)

    def paired(value, sends):
        return (value,), (swapped(value, sends),)

    def joined(of_near, of_cross):
        first = paired(of_near, near)
        second = paired(of_cross, cross)
        return tuple(a + b for a, b in zip(first, second))

    own_row = lax.dynamic_index_in_dim(pattern, row, 0, keepdims=True)

    def biases(*candidates):
        table = [[given.get(r, len(OFFSETS)) for given in candidates] for r in range(rows)]
        picks = jnp.asarray(table, jnp.int32)[row]
        here = jnp.arange(len(OFFSETS), dtype=jnp.int32)[None, :] == picks[:, None]
        live = jnp.sum(jnp.where(here, own_row, 0), axis=1)
        return jnp.where(live == 1, 0.0, FAR_BELOW).astype(jnp.float32)

    cut = values.shape[1] // PARTS
    visitors = moved(queries, near)
    k_far = [moved(keys, way[0]) for way in far]
    k_cross = moved(keys, cross)
    k_near = moved(keys, near)
    v_cross = moved(values, cross)
    v_near = moved(values, near)
    k_own, v_own = paired(keys, None), paired(values, None)

    result, stats = attend(None, visitors, [k_own], v_own, queries.dtype)
    visited = (moved(result, back), moved(stats, back))

    k_pairs = [k_own, joined(k_near, k_cross)]
    k_pairs += [paired(k, way[0]) for k, way in zip(k_far, far)]
    bias = biases(side, *[way[1] for way in far])
    base, of_side, *weights, stats = attend(bias, queries, k_pairs, v_own, jnp.float32)
    v_side = joined(v_near, v_cross)
    base, share = mix(biases(visit), base, of_side, v_side, stats, *visited)
    out = None
    for part in range(PARTS):
        here = values[:, part * cut : (part + 1) * cut]
        v_pairs = []
        for way in far:
            v = moved(here, way[0])
            v_pairs.append(paired(v, way[0]))
        out = finish(part, PARTS, base, share, weights, v_pairs, queries.dtype, out)
    return out


def solution(mesh):
    placed = P(("groups", "row", "col"), None)
    routes = plan(mesh.shape["row"])

    def body(*args):
        return shards(routes, *args)

    return jax.shard_map(
        body,
        mesh=mesh,
        in_specs=(placed, placed, placed, P("groups", None)),
        out_specs=placed,
        check_vma=False,
    )
```
